32 devices in a mesh: tok: 4 (over z), col: 8 (over y, x, core).
Axes of the slice: x: 2, y: 2, z: 4, core: 2. Of those that a mesh axis runs over, the one named last changes fastest.
Arguments:
- activations: bfloat16 [1024, 4096], P('tok'), may hold values from -6 to 6
- out_grad: bfloat16 [1024, 8192], P('tok', 'col'), may hold values from -0.1875 to 0.1875
- owned_blocks: int32 [4, 8, 5], P('tok'), may hold values from -1 to 127, as said below
- gram_left: float32 [4, 8, 5, 512, 512], P('tok', 'col'), may hold values from -6144 to 6656, as said below
- gram_right: float32 [4, 8, 5, 512, 512], P('tok', 'col'), may hold values from -6144 to 6656, as said below
Outputs:
- precond: bfloat16 [4096, 8192], P('tok', 'col')
- left_new: float32 [4, 8, 5, 512, 512], P('tok', 'col')
- right_new: float32 [4, 8, 5, 512, 512], P('tok', 'col')
The draws below stay inside these ranges and needn't reach their ends.
Inputs may be any that keep to these rules, and one draw needn't show every extreme that they name: owned_blocks[t] lists every block whose rows lie in rows t * 2 * 512 to (t + 1) * 2 * 512 - 1 exactly once; each device lists its block ids in ascending order followed by -1; the blocks of one device lie in pairwise different block columns; in each t some device fills all 5 slots. `gram_left`: each slot holds a symmetric positive definite matrix with eigenvalues of at least 256. `gram_right`: each slot holds a symmetric positive definite matrix with eigenvalues of at least 256.
All inputs are finite; a program needn't handle non-finite values.
Results may differ from the reference program's by a relative error of at most 0.015.
Values may be sent and summed in bfloat16 or wider, within the bound.
A program may use at most 128 MiB of HBM per device.

```python
import jax
import jax.numpy as jnp
from jax import lax

D = 8192
DI = 4096
B = 512
ITERS = 2
TOKENS = 1024
COL_BLOCKS = 16
ROW_BLOCKS = 2
SLOTS = 5
N_TOK = 4
N_COL = 8


def group_owners(key, group_index):
    mean_load = ROW_BLOCKS * COL_BLOCKS // N_COL
    spare_slots = SLOTS - mean_load
    sentinel = N_TOK * ROW_BLOCKS * COL_BLOCKS
    subkeys = jax.random.split(key, 4)
    lift_sizes = jax.random.randint(subkeys[0], (N_COL // 2,), 0, spare_slots + 1)
    lift_sizes = lift_sizes.at[0].set(spare_slots)
    load_counts = jnp.concatenate([mean_load - lift_sizes, mean_load + lift_sizes])
    load_counts = load_counts[jax.random.permutation(subkeys[1], N_COL)]
    starts = jnp.cumsum(load_counts) - load_counts
    positions = jnp.arange(SLOTS)
    rank_table = jnp.minimum(starts[:, None] + positions[None, :], ROW_BLOCKS * COL_BLOCKS - 1)
    filled = positions[None, :] < load_counts[:, None]
    row_order = jax.random.permutation(subkeys[2], ROW_BLOCKS)
    col_order = jax.random.permutation(subkeys[3], COL_BLOCKS)
    block_ids = (group_index * ROW_BLOCKS + row_order[rank_table // COL_BLOCKS]) * COL_BLOCKS + col_order[rank_table % COL_BLOCKS]
    marked = jnp.where(filled, block_ids, sentinel)
    ordered = jnp.sort(marked, axis=1)
    return jnp.where(ordered >= sentinel, -1, ordered).astype(jnp.int32)


def draw_owned_blocks(key, part):
    return jnp.stack([group_owners(jax.random.fold_in(key, 101 + group_index), group_index) for group_index in range(N_TOK)])


def gram_draw(key):
    total = N_TOK * N_COL * SLOTS

    def one_matrix(subkey):
        factor = jax.random.normal(subkey, (B, B), jnp.float32)
        product = jnp.dot(factor, factor.T, precision=lax.Precision.HIGHEST)
        return product + 0.5 * B * jnp.eye(B, dtype=jnp.float32)
    matrices = lax.map(one_matrix, jax.random.split(key, total))
    return matrices.reshape(N_TOK, N_COL, SLOTS, B, B)


def draw_gram_left(key, part):
    return gram_draw(jax.random.fold_in(key, 11))


def draw_gram_right(key, part):
    return gram_draw(jax.random.fold_in(key, 23))


def block_scale(key, shape, shards, smallest, high):
    loudness, own = 1.0, jax.random.fold_in(key, 6)
    for axis_at, shards_of in shards:
        steps = jnp.exp(jax.random.uniform(jax.random.fold_in(own, axis_at), (shards_of,), jnp.float32, smallest / len(shards), high / len(shards)))
        loudness = loudness * jnp.repeat(steps, shape[axis_at] // shards_of).reshape([-1 if axis == axis_at else 1 for axis in range(len(shape))])
    return loudness


def noise(key, extent, scale, reach, cuts=(), kind=jnp.bfloat16):
    drawn = scale * jax.random.normal(key, extent, jnp.float32)
    if cuts:
        drawn = drawn * block_scale(key, extent, cuts, -0.22, 0.18)
    return jnp.clip(drawn, -reach, reach).astype(kind)


def setup_inputs(seed: int = 0) -> dict:
    key_of = jax.random.split(jax.random.key(seed), 6)
    activations = noise(key_of[0], (TOKENS, DI), 1.0, 6.0, ((0, 4),))
    out_grad = noise(key_of[1], (TOKENS, D), TOKENS ** -0.5, 0.1875, ((0, 4), (1, 8)))
    owned_blocks = draw_owned_blocks(jax.random.fold_in(key_of[5], 71), 0)
    gram_left = draw_gram_left(jax.random.fold_in(key_of[5], 71), 0)
    gram_right = draw_gram_right(jax.random.fold_in(key_of[5], 71), 0)
    return {"activations": activations, "out_grad": out_grad, "owned_blocks": owned_blocks, "gram_left": gram_left, "gram_right": gram_right}


highest = lax.Precision.HIGHEST
decay_rate = 0.9
epsilon = 1e-06

def inverse_root(matrix):
    side = matrix.shape[-1]
    identity = jnp.eye(side, dtype=jnp.float32)
    mean_diag = jnp.trace(matrix, axis1=-2, axis2=-1) / side
    coupled = matrix / mean_diag[..., None, None]
    root = identity
    for iteration in range(ITERS):
        factor = (5.0 * identity - coupled) * 0.25
        if iteration == 0:
            root = factor
        else:
            root = jnp.einsum('...ij,...jk->...ik', root, factor, precision=highest)
        if iteration + 1 < ITERS:
            squared = jnp.einsum('...ij,...jk->...ik', factor, factor, precision=highest)
            fourth = jnp.einsum('...ij,...jk->...ik', squared, squared, precision=highest)
            coupled = jnp.einsum('...ij,...jk->...ik', fourth, coupled, precision=highest)
    return root

def reference(activations, out_grad, owned_blocks, gram_left, gram_right):
    gradient = jnp.dot(activations.T, out_grad, preferred_element_type=jnp.float32).astype(jnp.bfloat16)
    col_blocks = D // B
    block_ids = owned_blocks.reshape(-1).astype(jnp.int32)
    lefts = gram_left.reshape(-1, B, B)
    rights = gram_right.reshape(-1, B, B)

    def per_slot(inputs):
        ident, left_old, right_old = inputs
        occupied = ident >= 0
        clamped = jnp.where(occupied, ident, 0)
        row_start = (clamped // col_blocks * B).astype(jnp.int32)
        col_start = (clamped % col_blocks * B).astype(jnp.int32)
        block = lax.dynamic_slice(gradient, (row_start, col_start), (B, B))
        grad_block = jnp.where(occupied, block.astype(jnp.float32), jnp.float32(0.0))
        left_next = jnp.where(occupied, decay_rate * left_old + jnp.dot(grad_block, grad_block.T, precision=highest), left_old)
        right_next = jnp.where(occupied, decay_rate * right_old + jnp.dot(grad_block.T, grad_block, precision=highest), right_old)
        root_left = inverse_root(left_next)
        root_right = inverse_root(right_next)
        shaped = jnp.dot(jnp.dot(root_left, grad_block, precision=highest), root_right, precision=highest)
        grad_norm = jnp.sqrt(jnp.sum(grad_block * grad_block) + epsilon)
        shaped_norm = jnp.sqrt(jnp.sum(shaped * shaped) + epsilon)
        result = (shaped * (grad_norm / shaped_norm)).astype(jnp.bfloat16)
        return (left_next, right_next, result)
    left_all, right_all, results = lax.map(per_slot, (block_ids, lefts, rights))

    def place(index, canvas):
        ident = block_ids[index]
        occupied = ident >= 0
        clamped = jnp.where(occupied, ident, 0)
        row_start = (clamped // col_blocks * B).astype(jnp.int32)
        col_start = (clamped % col_blocks * B).astype(jnp.int32)
        present = lax.dynamic_slice(canvas, (row_start, col_start), (B, B))
        update = jnp.where(occupied, results[index], present)
        return lax.dynamic_update_slice(canvas, update, (row_start, col_start))
    precond = lax.fori_loop(0, block_ids.shape[0], place, jnp.zeros((DI, D), jnp.bfloat16))
    return (precond, left_all.reshape(gram_left.shape), right_all.reshape(gram_right.shape))
```

```python
import functools

import jax
import jax.numpy as jnp
from jax import lax
from jax.experimental import pallas as pl
from jax.experimental.pallas import tpu as pltpu
from jax.sharding import PartitionSpec as P

B = 512
decay_rate = 0.9
epsilon = 1e-06
f32 = jnp.float32
bf16 = jnp.bfloat16
MESH = pl.DeviceIdType.MESH
VMEM = pl.BlockSpec(memory_space=pltpu.VMEM)
ANY = pl.BlockSpec(memory_space=pl.ANY)
MIB = 1024 * 1024


def mm(a, b):
    return jnp.dot(a.astype(bf16), b.astype(bf16), preferred_element_type=f32)


def table_kernel(table, pick_ref, *, slots, row_blocks, col_count, col_blocks):
    base = lax.axis_index("tok") * (row_blocks * col_blocks)

    @pl.loop(0, col_count)
    def _(o):
        for s in range(slots):
            owned = table[o * slots + s]
            place = jnp.where(owned >= 0, owned - base, row_blocks * col_blocks)
            pick_ref[place] = o * slots + s


def root_minus_identity(matrix, diagonal):
    side = matrix.shape[-1]
    scale = 0.25 * side / jnp.sum(jnp.where(diagonal, matrix, 0.0))
    e = jnp.where(diagonal, 0.25, 0.0) - matrix * scale
    eb = e.astype(bf16)
    w = 2.0 * e + mm(eb, eb)
    v = w + e + mm(eb, w)
    r = v - 1.25 * w
    return (1.25 * e + r - 0.25 * v + mm(v, r)).astype(bf16)


def slot_math(gt, left_old, right_old, decay):
    g = gt.T
    rows = lax.broadcasted_iota(jnp.int32, (B, B), 0)
    cols = lax.broadcasted_iota(jnp.int32, (B, B), 1)
    diagonal = rows == cols
    left = decay * left_old + jnp.dot(g, gt, preferred_element_type=f32)
    right = decay * right_old + jnp.dot(gt, g, preferred_element_type=f32)
    yl = root_minus_identity(left, diagonal)
    yr = root_minus_identity(right, diagonal)
    g32 = g.astype(f32)
    first = g32 + jnp.dot(yl, g, preferred_element_type=f32)
    shaped = first + mm(first, yr)
    grad_norm = jnp.sqrt(jnp.sum(g32 * g32, keepdims=True) + epsilon)
    shaped_norm = jnp.sqrt(jnp.sum(shaped * shaped, keepdims=True) + epsilon)
    return (shaped * (grad_norm / shaped_norm)).astype(bf16), left, right


def main_kernel(
    slots,
    table,
    pick_ref,
    og_ref,
    act_ref,
    left_ref,
    right_ref,
    home_ref,
    left_out,
    right_out,
    og_in,
    og_turned,
    og_buf,
    act_buf,
    grad,
    send,
    got,
    back,
    returned,
    leaving,
    og_sems,
    act_sems,
    share_sems,
    partner_sems,
    z_sems,
    g_sems,
    last_sems,
    back_sems,
    home_sems,
    load_sems,
    keep_sems,
    local_sems,
):
    t = lax.axis_index("tok")
    c = lax.axis_index("col")
    tok_count, chunks, col_count, per_home, rows_q, _ = og_buf.shape
    chips = col_count // 2
    core = lax.rem(c, 2)
    chip = c // 2
    partner = chip * 2 + 1 - core
    row_blocks, width = home_ref.shape[0], home_ref.shape[3]
    col_blocks = grad.shape[0] // row_blocks
    per_block = got.shape[1]
    rows_home = act_buf.shape[4]
    base = t * (row_blocks * col_blocks)
    last = chunks - 1

    barrier = pltpu.get_barrier_semaphore()
    for d in range(1, col_count):
        pl.semaphore_signal(
            barrier, inc=1, device_id=(t, lax.rem(c + d, col_count)), device_id_type=MESH
        )
    for d in range(1, tok_count):
        pl.semaphore_signal(
            barrier, inc=1, device_id=(lax.rem(t + d, tok_count), c), device_id_type=MESH
        )

    def remote(src, dst, sent, received, to):
        return pltpu.make_async_remote_copy(
            src_ref=src,
            dst_ref=dst,
            send_sem=sent,
            recv_sem=received,
            device_id=to,
            device_id_type=MESH,
        )

    def other(d):
        return lax.rem(c + d, col_count)

    def load(side, s):
        source = (left_ref, right_ref)[side]
        target = (left_out, right_out)[side]
        return pltpu.make_async_copy(source.at[s], target.at[s], load_sems.at[side, s])

    def act_columns(to):
        return pl.ds(pl.multiple_of(to * rows_home, rows_home), rows_home)

    og_load = pltpu.make_async_copy(og_ref, og_in, local_sems.at[0])
    og_load.start()
    own_act = pltpu.make_async_copy(
        act_ref.at[:, :, :, act_columns(t)], act_buf.at[t], local_sems.at[1]
    )
    own_act.start()
    for s in range(slots):
        load(0, s).start()
        load(1, s).start()

    og_load.wait()
    og_turned[...] = og_in[...].T.reshape(og_turned.shape)
    pl.semaphore_wait(barrier, col_count + tok_count - 2)

    def act_copy(source, d):
        to = lax.rem(source + d, tok_count)
        return remote(
            act_ref.at[chip, core, :, act_columns(to)],
            act_buf.at[source, chip, core],
            act_sems.at[0, d],
            act_sems.at[1, source],
            (to, c),
        )

    def act_wait(d):
        source = lax.rem(t + d, tok_count)
        piece = act_buf.at[source, chip, core]
        remote(piece, piece, act_sems.at[0, d], act_sems.at[1, source], (source, c)).wait_recv()

    def share(d, m, held):
        token = lax.rem(t + d, tok_count)
        piece = act_buf.at[token, held, core]
        to = lax.rem(chip + m, chips) * 2 + core
        return remote(
            piece, piece, share_sems.at[0, d, m], share_sems.at[1, d, held], (t, to)
        )

    def share_wait(d, m):
        share(d, m, lax.rem(chip + m, chips)).wait_recv()

    def to_partner(d, lane):
        token = lax.rem(t + d, tok_count)
        half = act_buf.at[token, :, lane]
        return remote(half, half, partner_sems.at[0, d], partner_sems.at[1, d], (t, partner))

    def og_copy(q, d, place):
        to = other(d)
        return remote(
            og_turned.at[:, to, q],
            og_buf.at[t, q, place],
            og_sems.at[q, 0, d],
            og_sems.at[q, 1, place],
            (t, to),
        )

    def along(origin, q, up):
        step = 1 if up else -1
        chunk = og_buf.at[origin, q]
        kind = 0 if up else 1
        return remote(
            chunk, chunk, z_sems.at[kind, q, 0, origin], z_sems.at[kind, q, 1, origin], (t + step, c)
        )

    def og_start(q):
        og_buf[t, q, c] = og_turned[:, c, q]
        for d in range(1, col_count):
            og_copy(q, d, c).start()

    def og_on(q):
        for d in range(1, col_count):
            og_copy(q, d, other(d)).wait_recv()

        @pl.when(t < tok_count - 1)
        def _():
            along(t, q, True).start()

        @pl.when(t > 0)
        def _():
            along(t, q, False).start()

    def relay(q):
        for d in range(1, tok_count):

            @pl.when(t >= d)
            def _():
                along(t - d, q, True).wait_recv()

                @pl.when(t < tok_count - 1)
                def _():
                    along(t - d, q, True).start()

            @pl.when(t + d < tok_count)
            def _():
                along(t + d, q, False).wait_recv()

                @pl.when(t > 0)
                def _():
                    along(t + d, q, False).start()

    def multiply(q):
        rows = col_count * per_home * rows_q
        total = sum(
            jnp.dot(
                og_buf[k, q].reshape(rows, og_buf.shape[5]),
                act_buf[k].reshape(og_buf.shape[5], rows_home),
                preferred_element_type=f32,
            )
            for k in range(tok_count)
        )
        for r in range(row_blocks):
            piece = total[:, r * B : (r + 1) * B].reshape(col_blocks, per_block, rows_q, B)
            grad[pl.ds(r * col_blocks, col_blocks)] = piece.astype(bf16)

    def pick_piece(q, o, s):
        owned = table[o * slots + s]
        piece = grad[jnp.maximum(owned - base, 0)]
        send[q, o, s] = jnp.where(owned >= 0, piece, jnp.zeros_like(piece))

    def g_copy(q, d, place):
        to = other(d)
        return remote(
            send.at[q, to],
            got.at[:, :, place, q],
            g_sems.at[q, 0, d],
            g_sems.at[q, 1, place],
            (t, to),
        )

    def g_keep(q):
        return pltpu.make_async_copy(send.at[q, c], got.at[:, :, c, q], keep_sems.at[0, q])

    def last_copy(s, d, place):
        to = other(d)
        return remote(
            send.at[last, to, s],
            got.at[s, :, place, last],
            last_sems.at[s, 0, d],
            last_sems.at[s, 1, place],
            (t, to),
        )

    def last_keep(s):
        return pltpu.make_async_copy(
            send.at[last, c, s], got.at[s, :, c, last], keep_sems.at[1, s]
        )

    for d in range(1, tok_count):
        act_copy(t, d).start()
    og_start(0)
    og_on(0)

    @pl.loop(1, chunks)
    def _(q):
        og_start(q)

    for d in range(1, tok_count):
        act_wait(d)
        for m in range(1, chips):
            share(d, m, chip).start()
    for d in range(1, tok_count):
        for m in range(1, chips):
            share_wait(d, m)
        to_partner(d, core).start()

    @pl.loop(0, chunks)
    def _(q):
        @pl.when(q < last)
        def _():
            og_on(q + 1)

        relay(q)

        @pl.when(q == 0)
        def _():
            own_act.wait()
            for d in range(1, tok_count):
                to_partner(d, 1 - core).wait_recv()

        multiply(q)

        @pl.when(q < last)
        def _():
            @pl.loop(1, col_count)
            def _(d):
                for s in range(slots):
                    pick_piece(q, other(d), s)
                g_copy(q, d, c).start()

            for s in range(slots):
                pick_piece(q, c, s)
            g_keep(q).start()

    @pl.loop(0, slots)
    def _(s):
        @pl.loop(1, col_count)
        def _(d):
            pick_piece(last, other(d), s)
            last_copy(s, d, c).start()

        pick_piece(last, c, s)
        last_keep(s).start()

    @pl.loop(0, last)
    def _(q):
        g_keep(q).wait()
        for d in range(1, col_count):
            g_copy(q, d, other(d)).wait_recv()

    def back_copy(s, d, place):
        to = other(d)
        return remote(
            back.at[s, to],
            returned.at[place * slots + s],
            back_sems.at[s, 0, d],
            back_sems.at[s, 1, place],
            (t, to),
        )

    def back_keep(s):
        return pltpu.make_async_copy(
            back.at[s, c], returned.at[c * slots + s], keep_sems.at[2, s]
        )

    @pl.loop(0, slots)
    def _(s):
        load(0, s).wait()
        load(1, s).wait()
        last_keep(s).wait()
        for d in range(1, col_count):
            last_copy(s, d, other(d)).wait_recv()
        decay = jnp.where(table[c * slots + s] >= 0, f32(decay_rate), f32(1.0))
        result, left, right = slot_math(got[s].reshape(B, B), left_out[s], right_out[s], decay)
        back[s] = result.reshape(back.shape[1:])
        left_out[s] = left
        right_out[s] = right
        for d in range(1, col_count):
            back_copy(s, d, c).start()
        back_keep(s).start()

    def home_copy(d, place):
        to = other(d)
        return remote(
            leaving.at[to], home_ref.at[:, place], home_sems.at[0, d], home_sems.at[1, place], (t, to)
        )

    @pl.loop(0, slots)
    def _(s):
        back_keep(s).wait()
        for d in range(1, col_count):
            back_copy(s, d, other(d)).wait_recv()

    block_width = width // per_home

    def fill(h, target):
        for p in range(per_home):
            piece_at = h * per_home + p
            for r in range(row_blocks):
                place = pick_ref[r * col_blocks + piece_at // per_block]
                block = returned[place]
                if per_block > 1:
                    part = lax.rem(piece_at, per_block)
                    parts = [block[:, k * width : (k + 1) * width] for k in range(per_block)]
                    block = parts[0]
                    for k in range(1, per_block):
                        block = jnp.where(part == k, parts[k], block)
                target[r, :, p * block_width : (p + 1) * block_width] = block

    @pl.loop(1, col_count)
    def _(d):
        fill(other(d), leaving.at[other(d)])
        home_copy(d, c).start()

    fill(c, home_ref.at[:, c])

    for d in range(1, tok_count):
        act_copy(t, d).wait_send()
        to_partner(d, core).wait_send()
        for m in range(1, chips):
            share(d, m, chip).wait_send()

    @pl.loop(0, chunks)
    def _(q):
        for d in range(1, col_count):
            og_copy(q, d, c).wait_send()
        for origin in range(tok_count):

            @pl.when((t >= origin) & (t < tok_count - 1))
            def _():
                along(origin, q, True).wait_send()

            @pl.when((t <= origin) & (t > 0))
            def _():
                along(origin, q, False).wait_send()

    @pl.loop(0, last)
    def _(q):
        for d in range(1, col_count):
            g_copy(q, d, c).wait_send()

    @pl.loop(0, slots)
    def _(s):
        for d in range(1, col_count):
            last_copy(s, d, c).wait_send()
            back_copy(s, d, c).wait_send()

    for d in range(1, col_count):
        home_copy(d, other(d)).wait_recv()
        home_copy(d, c).wait_send()


def place_kernel(in_ref, left_ref, right_ref, out_ref, left_out, right_out, sems):
    copies = [
        pltpu.make_async_copy(left_ref, left_out, sems.at[0]),
        pltpu.make_async_copy(right_ref, right_out, sems.at[1]),
        pltpu.make_async_copy(in_ref, out_ref, sems.at[2]),
    ]
    for copy in copies:
        copy.start()
    for copy in copies:
        copy.wait()


def per_device(activations, out_grad, owned_blocks, gram_left, gram_right):
    tok_count = lax.axis_size("tok")
    col_count = lax.axis_size("col")
    tok_local, shard_width = out_grad.shape
    rows_home = activations.shape[1] // tok_count
    row_blocks = rows_home // B
    col_blocks = shard_width * col_count // B
    piece_width = min(B, shard_width)
    per_home = shard_width // piece_width
    per_block = B // piece_width
    sub = piece_width // col_count
    chunks = max(1, sub // 16)
    rows_q = sub // chunks
    back_rows = B // col_count
    owners = owned_blocks[0]
    slots = owners.shape[1]
    table = owners.reshape(-1)
    smem = pl.BlockSpec(memory_space=pltpu.SMEM)
    pick = pl.pallas_call(
        functools.partial(
            table_kernel,
            slots=slots,
            row_blocks=row_blocks,
            col_count=col_count,
            col_blocks=col_blocks,
        ),
        out_shape=jax.ShapeDtypeStruct((row_blocks * col_blocks + 1,), jnp.int32),
        in_specs=[smem],
        out_specs=smem,
    )(table)

    act = activations.reshape(col_count // 2, 2, tok_local // col_count, activations.shape[1])
    sem = pltpu.SemaphoreType.DMA
    out, left_next, right_next = pl.pallas_call(
        functools.partial(main_kernel, slots),
        out_shape=[
            jax.ShapeDtypeStruct((row_blocks, col_count, back_rows, shard_width), bf16),
            jax.ShapeDtypeStruct((slots, B, B), f32),
            jax.ShapeDtypeStruct((slots, B, B), f32),
        ],
        in_specs=[smem, smem, ANY, ANY, ANY, ANY],
        out_specs=[VMEM, VMEM, VMEM],
        scratch_shapes=[
            pltpu.VMEM((tok_local, shard_width), bf16),
            pltpu.VMEM((per_home, col_count, chunks, rows_q, tok_local), bf16),
            pltpu.VMEM((tok_count, chunks, col_count, per_home, rows_q, tok_local), bf16),
            pltpu.VMEM(
                (tok_count, col_count // 2, 2, tok_local // col_count, rows_home), bf16
            ),
            pltpu.VMEM((row_blocks * col_blocks, per_block, rows_q, B), bf16),
            pltpu.VMEM((chunks, col_count, slots, per_block, rows_q, B), bf16),
            pltpu.VMEM((slots, per_block, col_count, chunks, rows_q, B), bf16),
            pltpu.VMEM((slots, col_count, back_rows, B), bf16),
            pltpu.VMEM((col_count * slots, back_rows, B), bf16),
            pltpu.VMEM((col_count, row_blocks, back_rows, shard_width), bf16),
            sem((chunks, 2, col_count)),
            sem((2, tok_count)),
            sem((2, tok_count, col_count // 2)),
            sem((2, tok_count)),
            sem((2, chunks, 2, tok_count)),
            sem((chunks, 2, col_count)),
            sem((slots, 2, col_count)),
            sem((slots, 2, col_count)),
            sem((2, col_count)),
            sem((2, slots)),
            sem((3, max(slots, chunks))),
            sem((2,)),
        ],
        compiler_params=pltpu.CompilerParams(
            collective_id=0, has_side_effects=True, vmem_limit_bytes=48 * MIB
        ),
    )(table, pick, out_grad, act, gram_left[0, 0], gram_right[0, 0])
    return tuple(
        pl.pallas_call(
            place_kernel,
            out_shape=[
                jax.ShapeDtypeStruct((rows_home, shard_width), bf16),
                jax.ShapeDtypeStruct((1, 1, slots, B, B), f32),
                jax.ShapeDtypeStruct((1, 1, slots, B, B), f32),
            ],
            in_specs=[VMEM, VMEM, VMEM],
            out_specs=[ANY, ANY, ANY],
            scratch_shapes=[pltpu.SemaphoreType.DMA((3,))],
            compiler_params=pltpu.CompilerParams(vmem_limit_bytes=16 * MIB),
        )(out.reshape(rows_home, shard_width), left_next[None, None], right_next[None, None])
    )


def solution(mesh):
    in_specs = (
        P("tok", None),
        P("tok", "col"),
        P("tok", None, None),
        P("tok", "col", None, None, None),
        P("tok", "col", None, None, None),
    )
    out_specs = (
        P("tok", "col"),
        P("tok", "col", None, None, None),
        P("tok", "col", None, None, None),
    )
    return jax.shard_map(
        per_device, mesh=mesh, in_specs=in_specs, out_specs=out_specs, check_vma=False
    )
```

```python
import functools

import jax
import jax.numpy as jnp
from jax import lax
from jax.experimental import pallas as pl
from jax.experimental.pallas import tpu as pltpu
from jax.sharding import PartitionSpec as P

B = 512
decay_rate = 0.9
epsilon = 1e-06
f32 = jnp.float32
bf16 = jnp.bfloat16
MESH = pl.DeviceIdType.MESH
VMEM = pl.BlockSpec(memory_space=pltpu.VMEM)
ANY = pl.BlockSpec(memory_space=pl.ANY)
MIB = 1024 * 1024


def mm(a, b):
    return jnp.dot(a.astype(bf16), b.astype(bf16), preferred_element_type=f32)


def root_minus_identity(matrix, diagonal):
    side = matrix.shape[-1]
    scale = 0.25 * side / jnp.sum(jnp.where(diagonal, matrix, 0.0))
    e = jnp.where(diagonal, 0.25, 0.0) - matrix * scale
    eb = e.astype(bf16)
    w = 2.0 * e + mm(eb, eb)
    v = w + e + mm(eb, w)
    r = v - 1.25 * w
    return (1.25 * e + r - 0.25 * v + mm(v, r)).astype(bf16)


def slot_math(gt, left_old, right_old, decay):
    g = gt.T
    rows = lax.broadcasted_iota(jnp.int32, (B, B), 0)
    cols = lax.broadcasted_iota(jnp.int32, (B, B), 1)
    diagonal = rows == cols
    left = decay * left_old + jnp.dot(g, gt, preferred_element_type=f32)
    right = decay * right_old + jnp.dot(gt, g, preferred_element_type=f32)
    yl = root_minus_identity(left, diagonal)
    yr = root_minus_identity(right, diagonal)
    g32 = g.astype(f32)
    first = g32 + jnp.dot(yl, g, preferred_element_type=f32)
    shaped = first + mm(first, yr)
    grad_norm = jnp.sqrt(jnp.sum(g32 * g32, keepdims=True) + epsilon)
    shaped_norm = jnp.sqrt(jnp.sum(shaped * shaped, keepdims=True) + epsilon)
    return (shaped * (grad_norm / shaped_norm)).astype(bf16), left, right


def main_kernel(
    slots,
    table,
    og_ref,
    act_ref,
    left_ref,
    right_ref,
    home_ref,
    left_out,
    right_out,
    og_in,
    og_turned,
    og_buf,
    act_buf,
    grad,
    send,
    got,
    back,
    returned,
    leaving,
    pick_ref,
    og_sems,
    act_sems,
    share_sems,
    partner_sems,
    z_sems,
    g_sems,
    last_sems,
    back_sems,
    home_sems,
    load_sems,
    keep_sems,
    local_sems,
):
    t = lax.axis_index("tok")
    c = lax.axis_index("col")
    tok_count, chunks, col_count, per_home, rows_q, _ = og_buf.shape
    chips = col_count // 2
    core = lax.rem(c, 2)
    chip = c // 2
    partner = chip * 2 + 1 - core
    row_blocks, width = home_ref.shape[0], home_ref.shape[3]
    col_blocks = grad.shape[0] // row_blocks
    per_block = got.shape[1]
    rows_home = act_buf.shape[4]
    base = t * (row_blocks * col_blocks)
    last = chunks - 1

    barrier = pltpu.get_barrier_semaphore()
    for d in range(1, col_count):
        pl.semaphore_signal(
            barrier, inc=1, device_id=(t, lax.rem(c + d, col_count)), device_id_type=MESH
        )
    for d in range(1, tok_count):
        pl.semaphore_signal(
            barrier, inc=1, device_id=(lax.rem(t + d, tok_count), c), device_id_type=MESH
        )

    def remote(src, dst, sent, received, to):
        return pltpu.make_async_remote_copy(
            src_ref=src,
            dst_ref=dst,
            send_sem=sent,
            recv_sem=received,
            device_id=to,
            device_id_type=MESH,
        )

    def other(d):
        return lax.rem(c + d, col_count)

    def load(side, s):
        source = (left_ref, right_ref)[side]
        target = (left_out, right_out)[side]
        return pltpu.make_async_copy(source.at[s], target.at[s], load_sems.at[side, s])

    def act_columns(to):
        return pl.ds(pl.multiple_of(to * rows_home, rows_home), rows_home)

    og_load = pltpu.make_async_copy(og_ref, og_in, local_sems.at[0])
    og_load.start()
    own_act = pltpu.make_async_copy(
        act_ref.at[:, :, :, act_columns(t)], act_buf.at[t], local_sems.at[1]
    )
    own_act.start()
    for s in range(slots):
        load(0, s).start()
        load(1, s).start()

    og_load.wait()
    og_turned[...] = og_in[...].T.reshape(og_turned.shape)
    pl.semaphore_wait(barrier, col_count + tok_count - 2)

    def act_copy(source, d):
        to = lax.rem(source + d, tok_count)
        return remote(
            act_ref.at[chip, core, :, act_columns(to)],
            act_buf.at[source, chip, core],
            act_sems.at[0, d],
            act_sems.at[1, source],
            (to, c),
        )

    def act_wait(d):
        source = lax.rem(t + d, tok_count)
        piece = act_buf.at[source, chip, core]
        remote(piece, piece, act_sems.at[0, d], act_sems.at[1, source], (source, c)).wait_recv()

    def share(d, m, held):
        token = lax.rem(t + d, tok_count)
        piece = act_buf.at[token, held, core]
        to = lax.rem(chip + m, chips) * 2 + core
        return remote(
            piece, piece, share_sems.at[0, d, m], share_sems.at[1, d, held], (t, to)
        )

    def share_wait(d, m):
        share(d, m, lax.rem(chip + m, chips)).wait_recv()

    def to_partner(d, lane):
        token = lax.rem(t + d, tok_count)
        half = act_buf.at[token, :, lane]
        return remote(half, half, partner_sems.at[0, d], partner_sems.at[1, d], (t, partner))

    def og_copy(q, d, place):
        to = other(d)
        return remote(
            og_turned.at[:, to, q],
            og_buf.at[t, q, place],
            og_sems.at[q, 0, d],
            og_sems.at[q, 1, place],
            (t, to),
        )

    def along(origin, q, up):
        step = 1 if up else -1
        chunk = og_buf.at[origin, q]
        kind = 0 if up else 1
        return remote(
            chunk, chunk, z_sems.at[kind, q, 0, origin], z_sems.at[kind, q, 1, origin], (t + step, c)
        )

    def og_start(q):
        og_buf[t, q, c] = og_turned[:, c, q]
        for d in range(1, col_count):
            og_copy(q, d, c).start()

    def og_on(q):
        for d in range(1, col_count):
            og_copy(q, d, other(d)).wait_recv()

        @pl.when(t < tok_count - 1)
        def _():
            along(t, q, True).start()

        @pl.when(t > 0)
        def _():
            along(t, q, False).start()

    def relay(q):
        for d in range(1, tok_count):

            @pl.when(t >= d)
            def _():
                along(t - d, q, True).wait_recv()

                @pl.when(t < tok_count - 1)
                def _():
                    along(t - d, q, True).start()

            @pl.when(t + d < tok_count)
            def _():
                along(t + d, q, False).wait_recv()

                @pl.when(t > 0)
                def _():
                    along(t + d, q, False).start()

    def multiply(q):
        rows = col_count * per_home * rows_q
        total = sum(
            jnp.dot(
                og_buf[k, q].reshape(rows, og_buf.shape[5]),
                act_buf[k].reshape(og_buf.shape[5], rows_home),
                preferred_element_type=f32,
            )
            for k in range(tok_count)
        )
        for r in range(row_blocks):
            piece = total[:, r * B : (r + 1) * B].reshape(col_blocks, per_block, rows_q, B)
            grad[pl.ds(r * col_blocks, col_blocks)] = piece.astype(bf16)

    def pick_piece(q, o, s):
        owned = table[s, o]
        piece = grad[jnp.maximum(owned - base, 0)]
        send[q, o, s] = jnp.where(owned >= 0, piece, jnp.zeros_like(piece))

    def g_copy(q, d, place):
        to = other(d)
        return remote(
            send.at[q, to],
            got.at[:, :, place, q],
            g_sems.at[q, 0, d],
            g_sems.at[q, 1, place],
            (t, to),
        )

    def g_keep(q):
        return pltpu.make_async_copy(send.at[q, c], got.at[:, :, c, q], keep_sems.at[0, q])

    def last_copy(s, d, place):
        to = other(d)
        return remote(
            send.at[last, to, s],
            got.at[s, :, place, last],
            last_sems.at[s, 0, d],
            last_sems.at[s, 1, place],
            (t, to),
        )

    def last_keep(s):
        return pltpu.make_async_copy(
            send.at[last, c, s], got.at[s, :, c, last], keep_sems.at[1, s]
        )

    edge = (t == 0) | (t == tok_count - 1)
    early = min(2, chunks)
    og_start(0)
    for d in range(1, tok_count):
        act_copy(t, d).start()
    for q in range(1, chunks):
        og_start(q)
    for q in range(early):
        og_on(q)

    for d in range(1, tok_count):
        act_wait(d)
        for m in range(1, chips):
            share(d, m, chip).start()

    @pl.when(edge)
    def _():
        for q in range(early, chunks):
            og_on(q)

    @pl.loop(0, row_blocks * col_blocks)
    def _(place):
        found = jnp.int32(0)
        for s in range(slots):
            for o in range(col_count):
                found = jnp.where(table[s, o] == base + place, o * slots + s, found)
        pick_ref[place] = found

    @pl.loop(0, chunks)
    def _(q):
        relay(q)

        @pl.when(q == 0)
        def _():
            for d in range(1, tok_count):
                for m in range(1, chips):
                    share_wait(d, m)
                to_partner(d, core).start()

        @pl.when(jnp.logical_not(edge) & (q + early < chunks))
        def _():
            og_on(q + early)

        @pl.when(q == 0)
        def _():
            own_act.wait()
            for d in range(1, tok_count):
                to_partner(d, 1 - core).wait_recv()

        multiply(q)

        @pl.when(q < last)
        def _():
            @pl.loop(1, col_count)
            def _(d):
                for s in range(slots):
                    pick_piece(q, other(d), s)
                g_copy(q, d, c).start()

            for s in range(slots):
                pick_piece(q, c, s)
            g_keep(q).start()

    def last_send(s):
        @pl.loop(1, col_count)
        def _(d):
            pick_piece(last, other(d), s)
            last_copy(s, d, c).start()

        pick_piece(last, c, s)
        last_keep(s).start()

    first = min(2, slots)

    @pl.loop(0, first)
    def _(s):
        last_send(s)

    @pl.loop(0, last)
    def _(q):
        g_keep(q).wait()
        for d in range(1, col_count):
            g_copy(q, d, other(d)).wait_recv()

    def back_copy(s, d, place):
        to = other(d)
        return remote(
            back.at[s, to],
            returned.at[place * slots + s],
            back_sems.at[s, 0, d],
            back_sems.at[s, 1, place],
            (t, to),
        )

    def back_keep(s):
        return pltpu.make_async_copy(
            back.at[s, c], returned.at[c * slots + s], keep_sems.at[2, s]
        )

    @pl.loop(0, slots)
    def _(s):
        load(0, s).wait()
        load(1, s).wait()
        last_keep(s).wait()
        for d in range(1, col_count):
            last_copy(s, d, other(d)).wait_recv()

        @pl.when(s == 0)
        def _():
            @pl.loop(first, slots)
            def _(later):
                last_send(later)

        decay = jnp.where(table[s, c] >= 0, f32(decay_rate), f32(1.0))
        result, left, right = slot_math(got[s].reshape(B, B), left_out[s], right_out[s], decay)
        back[s] = result.reshape(back.shape[1:])
        left_out[s] = left
        right_out[s] = right
        for d in range(1, col_count):
            back_copy(s, d, c).start()
        back_keep(s).start()

    def home_copy(d, place):
        to = other(d)
        return remote(
            leaving.at[to], home_ref.at[:, place], home_sems.at[0, d], home_sems.at[1, place], (t, to)
        )

    @pl.loop(0, slots)
    def _(s):
        back_keep(s).wait()
        for d in range(1, col_count):
            back_copy(s, d, other(d)).wait_recv()

    block_width = width // per_home

    def fill(h, target):
        for p in range(per_home):
            piece_at = h * per_home + p
            for r in range(row_blocks):
                place = pick_ref[r * col_blocks + piece_at // per_block]
                block = returned[place]
                if per_block > 1:
                    part = lax.rem(piece_at, per_block)
                    parts = [block[:, k * width : (k + 1) * width] for k in range(per_block)]
                    block = parts[0]
                    for k in range(1, per_block):
                        block = jnp.where(part == k, parts[k], block)
                target[r, :, p * block_width : (p + 1) * block_width] = block

    @pl.loop(1, col_count)
    def _(d):
        fill(other(d), leaving.at[other(d)])
        home_copy(d, c).start()

    fill(c, home_ref.at[:, c])

    for d in range(1, tok_count):
        act_copy(t, d).wait_send()
        to_partner(d, core).wait_send()
        for m in range(1, chips):
            share(d, m, chip).wait_send()

    @pl.loop(0, chunks)
    def _(q):
        for d in range(1, col_count):
            og_copy(q, d, c).wait_send()
        for origin in range(tok_count):

            @pl.when((t >= origin) & (t < tok_count - 1))
            def _():
                along(origin, q, True).wait_send()

            @pl.when((t <= origin) & (t > 0))
            def _():
                along(origin, q, False).wait_send()

    @pl.loop(0, last)
    def _(q):
        for d in range(1, col_count):
            g_copy(q, d, c).wait_send()

    @pl.loop(0, slots)
    def _(s):
        for d in range(1, col_count):
            last_copy(s, d, c).wait_send()
            back_copy(s, d, c).wait_send()

    for d in range(1, col_count):
        home_copy(d, other(d)).wait_recv()
        home_copy(d, c).wait_send()


def place_kernel(in_ref, left_ref, right_ref, out_ref, left_out, right_out, sems):
    copies = [
        pltpu.make_async_copy(left_ref, left_out, sems.at[0]),
        pltpu.make_async_copy(right_ref, right_out, sems.at[1]),
        pltpu.make_async_copy(in_ref, out_ref, sems.at[2]),
    ]
    for copy in copies:
        copy.start()
    for copy in copies:
        copy.wait()


def per_device(activations, out_grad, owned_blocks, gram_left, gram_right):
    tok_count = lax.axis_size("tok")
    col_count = lax.axis_size("col")
    tok_local, shard_width = out_grad.shape
    rows_home = activations.shape[1] // tok_count
    row_blocks = rows_home // B
    col_blocks = shard_width * col_count // B
    piece_width = min(B, shard_width)
    per_home = shard_width // piece_width
    per_block = B // piece_width
    sub = piece_width // col_count
    chunks = max(1, sub // 16)
    rows_q = sub // chunks
    back_rows = B // col_count
    owners = owned_blocks[0]
    slots = owners.shape[1]
    smem = pl.BlockSpec(memory_space=pltpu.SMEM)

    act = activations.reshape(col_count // 2, 2, tok_local // col_count, activations.shape[1])
    sem = pltpu.SemaphoreType.DMA
    out, left_next, right_next = pl.pallas_call(
        functools.partial(main_kernel, slots),
        out_shape=[
            pltpu.VMEM((row_blocks, col_count, back_rows, shard_width), bf16),
            pltpu.VMEM((slots, B, B), f32),
            pltpu.VMEM((slots, B, B), f32),
        ],
        in_specs=[smem, ANY, ANY, ANY, ANY],
        out_specs=[VMEM, VMEM, VMEM],
        scratch_shapes=[
            pltpu.VMEM((tok_local, shard_width), bf16),
            pltpu.VMEM((per_home, col_count, chunks, rows_q, tok_local), bf16),
            pltpu.VMEM((tok_count, chunks, col_count, per_home, rows_q, tok_local), bf16),
            pltpu.VMEM(
                (tok_count, col_count // 2, 2, tok_local // col_count, rows_home), bf16
            ),
            pltpu.VMEM((row_blocks * col_blocks, per_block, rows_q, B), bf16),
            pltpu.VMEM((chunks, col_count, slots, per_block, rows_q, B), bf16),
            pltpu.VMEM((slots, per_block, col_count, chunks, rows_q, B), bf16),
            pltpu.VMEM((slots, col_count, back_rows, B), bf16),
            pltpu.VMEM((col_count * slots, back_rows, B), bf16),
            pltpu.VMEM((col_count, row_blocks, back_rows, shard_width), bf16),
            pltpu.SMEM((row_blocks * col_blocks,), jnp.int32),
            sem((chunks, 2, col_count)),
            sem((2, tok_count)),
            sem((2, tok_count, col_count // 2)),
            sem((2, tok_count)),
            sem((2, chunks, 2, tok_count)),
            sem((chunks, 2, col_count)),
            sem((slots, 2, col_count)),
            sem((slots, 2, col_count)),
            sem((2, col_count)),
            sem((2, slots)),
            sem((3, max(slots, chunks))),
            sem((2,)),
        ],
        compiler_params=pltpu.CompilerParams(
            collective_id=0, has_side_effects=True, vmem_limit_bytes=48 * MIB
        ),
    )(
        owners.T,
        *(
            pltpu.with_memory_space_constraint(x, pltpu.HBM)
            for x in (out_grad, act, gram_left[0, 0], gram_right[0, 0])
        ),
    )
    return tuple(
        pl.pallas_call(
            place_kernel,
            out_shape=[
                jax.ShapeDtypeStruct((rows_home, shard_width), bf16),
                jax.ShapeDtypeStruct((1, 1, slots, B, B), f32),
                jax.ShapeDtypeStruct((1, 1, slots, B, B), f32),
            ],
            in_specs=[VMEM, VMEM, VMEM],
            out_specs=[ANY, ANY, ANY],
            scratch_shapes=[pltpu.SemaphoreType.DMA((3,))],
            compiler_params=pltpu.CompilerParams(vmem_limit_bytes=16 * MIB),
        )(out.reshape(rows_home, shard_width), left_next[None, None], right_next[None, None])
    )


def solution(mesh):
    in_specs = (
        P("tok", None),
        P("tok", "col"),
        P("tok", None, None),
        P("tok", "col", None, None, None),
        P("tok", "col", None, None, None),
    )
    out_specs = (
        P("tok", "col"),
        P("tok", "col", None, None, None),
        P("tok", "col", None, None, None),
    )
    return jax.shard_map(
        per_device, mesh=mesh, in_specs=in_specs, out_specs=out_specs, check_vma=False
    )
```

```python
import functools

import jax
import jax.numpy as jnp
from jax import lax
from jax.experimental import pallas as pl
from jax.experimental.pallas import tpu as pltpu
from jax.sharding import PartitionSpec as P

B = 512
decay_rate = 0.9
epsilon = 1e-06
f32 = jnp.float32
bf16 = jnp.bfloat16
MESH = pl.DeviceIdType.MESH
VMEM = pl.BlockSpec(memory_space=pltpu.VMEM)
ANY = pl.BlockSpec(memory_space=pl.ANY)
MIB = 1024 * 1024


def mm(a, b):
    return jnp.dot(a.astype(bf16), b.astype(bf16), preferred_element_type=f32)


def root_minus_identity(matrix, diagonal):
    side = matrix.shape[-1]
    scale = 0.25 * side / jnp.sum(jnp.where(diagonal, matrix, 0.0))
    e = jnp.where(diagonal, 0.25, 0.0) - matrix * scale
    eb = e.astype(bf16)
    w = 2.0 * e + mm(eb, eb)
    v = w + e + mm(eb, w)
    r = v - 1.25 * w
    return (1.25 * e + r - 0.25 * v + mm(v, r)).astype(bf16)


def slot_math(gt, left_old, right_old, decay):
    g = gt.T
    rows = lax.broadcasted_iota(jnp.int32, (B, B), 0)
    cols = lax.broadcasted_iota(jnp.int32, (B, B), 1)
    diagonal = rows == cols
    left = decay * left_old + jnp.dot(g, gt, preferred_element_type=f32)
    right = decay * right_old + jnp.dot(gt, g, preferred_element_type=f32)
    yl = root_minus_identity(left, diagonal)
    yr = root_minus_identity(right, diagonal)
    g32 = g.astype(f32)
    first = g32 + jnp.dot(yl, g, preferred_element_type=f32)
    shaped = first + mm(first, yr)
    grad_norm = jnp.sqrt(jnp.sum(g32 * g32, keepdims=True) + epsilon)
    shaped_norm = jnp.sqrt(jnp.sum(shaped * shaped, keepdims=True) + epsilon)
    return (shaped * (grad_norm / shaped_norm)).astype(bf16), left, right


def main_kernel(
    slots,
    table,
    og_ref,
    act_ref,
    left_ref,
    right_ref,
    home_ref,
    left_out,
    right_out,
    og_in,
    og_turned,
    og_buf,
    act_buf,
    grad,
    send,
    got,
    back,
    returned,
    leaving,
    pick_ref,
    send_sems,
    og_sems,
    act_sems,
    share_sems,
    partner_sems,
    z_sems,
    g_sems,
    last_sems,
    back_sems,
    home_sems,
    local_sems,
):
    t = lax.axis_index("tok")
    c = lax.axis_index("col")
    tok_count, chunks, col_count, per_home, rows_q, _ = og_buf.shape
    chips = col_count // 2
    core = lax.rem(c, 2)
    chip = c // 2
    partner = chip * 2 + 1 - core
    row_blocks, width = home_ref.shape[0], home_ref.shape[3]
    col_blocks = grad.shape[0] // row_blocks
    per_block = got.shape[1]
    rows_home = act_buf.shape[4]
    base = t * (row_blocks * col_blocks)
    last = chunks - 1

    barrier = pltpu.get_barrier_semaphore()
    for d in range(1, col_count):
        pl.semaphore_signal(
            barrier, inc=1, device_id=(t, lax.rem(c + d, col_count)), device_id_type=MESH
        )
    for d in range(1, tok_count):
        pl.semaphore_signal(
            barrier, inc=1, device_id=(lax.rem(t + d, tok_count), c), device_id_type=MESH
        )

    def remote(src, dst, sent, received, to):
        return pltpu.make_async_remote_copy(
            src_ref=src,
            dst_ref=dst,
            send_sem=sent,
            recv_sem=received,
            device_id=to,
            device_id_type=MESH,
        )

    def arrived(size, sem):
        remote(size, size, sem, sem, (t, partner)).wait_recv()

    def gone(size, sem):
        remote(size, size, sem, sem, (t, partner)).wait_send()

    def other(d):
        return lax.rem(c + d, col_count)

    loads = [
        pltpu.make_async_copy(left_ref, left_out, local_sems.at[2]),
        pltpu.make_async_copy(right_ref, right_out, local_sems.at[3]),
    ]

    def act_columns(to):
        return pl.ds(pl.multiple_of(to * rows_home, rows_home), rows_home)

    og_load = pltpu.make_async_copy(og_ref, og_in, local_sems.at[0])
    og_load.start()
    own_act = pltpu.make_async_copy(
        act_ref.at[:, :, :, act_columns(t)], act_buf.at[t], local_sems.at[1]
    )
    own_act.start()
    for load in loads:
        load.start()

    og_load.wait()
    og_turned[...] = og_in[...].T.reshape(og_turned.shape)
    pl.semaphore_wait(barrier, col_count + tok_count - 2)

    def act_copy(source, d):
        to = lax.rem(source + d, tok_count)
        return remote(
            act_ref.at[chip, core, :, act_columns(to)],
            act_buf.at[source, chip, core],
            send_sems.at[0],
            act_sems.at[source],
            (to, c),
        )

    def act_wait(d):
        source = lax.rem(t + d, tok_count)
        piece = act_buf.at[source, chip, core]
        arrived(piece, act_sems.at[source])

    def share(d, m, held):
        token = lax.rem(t + d, tok_count)
        piece = act_buf.at[token, held, core]
        to = lax.rem(chip + m, chips) * 2 + core
        return remote(piece, piece, send_sems.at[1], share_sems.at[d], (t, to))

    def to_partner(d, lane):
        token = lax.rem(t + d, tok_count)
        half = act_buf.at[token, :, lane]
        return remote(half, half, send_sems.at[2], partner_sems.at[d], (t, partner))

    def og_copy(q, d, place):
        to = other(d)
        return remote(
            og_turned.at[:, to, q],
            og_buf.at[t, q, place],
            send_sems.at[3],
            og_sems.at[q],
            (t, to),
        )

    def along(origin, q, up):
        step = 1 if up else -1
        chunk = og_buf.at[origin, q]
        kind = 0 if up else 1
        return remote(
            chunk, chunk, send_sems.at[4 + kind], z_sems.at[q, origin], (t + step, c)
        )

    def og_start(q):
        og_buf[t, q, c] = og_turned[:, c, q]
        for d in range(1, col_count):
            og_copy(q, d, c).start()

    def og_on(q):
        arrived(og_turned.at[:, 0 : col_count - 1, q], og_sems.at[q])

        @pl.when(t < tok_count - 1)
        def _():
            along(t, q, True).start()

        @pl.when(t > 0)
        def _():
            along(t, q, False).start()

    def relay(q):
        for d in range(1, tok_count):

            @pl.when(t >= d)
            def _():
                along(t - d, q, True).wait_recv()

                @pl.when(t < tok_count - 1)
                def _():
                    along(t - d, q, True).start()

            @pl.when(t + d < tok_count)
            def _():
                along(t + d, q, False).wait_recv()

                @pl.when(t > 0)
                def _():
                    along(t + d, q, False).start()

    def multiply(q):
        rows = col_count * per_home * rows_q
        total = sum(
            jnp.dot(
                og_buf[k, q].reshape(rows, og_buf.shape[5]),
                act_buf[k].reshape(og_buf.shape[5], rows_home),
                preferred_element_type=f32,
            )
            for k in range(tok_count)
        )
        for r in range(row_blocks):
            piece = total[:, r * B : (r + 1) * B].reshape(col_blocks, per_block, rows_q, B)
            grad[pl.ds(r * col_blocks, col_blocks)] = piece.astype(bf16)

    def pick_piece(o, s):
        owned = table[s, 0, o]
        piece = grad[jnp.maximum(owned - base, 0)]
        return jnp.where(owned >= 0, piece, jnp.zeros_like(piece))

    def g_copy(q, d, place):
        to = other(d)
        return remote(
            send.at[q, to],
            got.at[:, :, place, q],
            send_sems.at[6],
            g_sems.at[q],
            (t, to),
        )

    def last_copy(s, d, place):
        to = other(d)
        return remote(
            send.at[last, to, s],
            got.at[s, :, place, last],
            send_sems.at[6],
            last_sems.at[s],
            (t, to),
        )

    edge = (t == 0) | (t == tok_count - 1)
    early = min(2, chunks)
    og_start(0)
    for d in range(1, tok_count):
        act_copy(t, d).start()
    for q in range(1, chunks):
        og_start(q)
    for q in range(early):
        og_on(q)

    for d in range(1, tok_count):
        act_wait(d)
        for m in range(1, chips):
            share(d, m, chip).start()

    @pl.when(edge)
    def _():
        for q in range(early, chunks):
            og_on(q)

    @pl.loop(0, row_blocks * col_blocks)
    def _(place):
        found = jnp.int32(0)
        for s in range(slots):
            for o in range(col_count):
                found = jnp.where(table[s, 0, o] == base + place, o * slots + s, found)
        pick_ref[place] = found

    @pl.loop(0, chunks)
    def _(q):
        relay(q)

        @pl.when(q == 0)
        def _():
            for d in range(1, tok_count):
                arrived(act_buf.at[0, 0 : chips - 1, 0], share_sems.at[d])
                to_partner(d, core).start()

        @pl.when(jnp.logical_not(edge) & (q + early < chunks))
        def _():
            og_on(q + early)

        @pl.when(q == 0)
        def _():
            own_act.wait()
            for d in range(1, tok_count):
                to_partner(d, 1 - core).wait_recv()

        multiply(q)

        @pl.when(q < last)
        def _():
            @pl.loop(1, col_count)
            def _(d):
                for s in range(slots):
                    send[q, other(d), s] = pick_piece(other(d), s)
                g_copy(q, d, c).start()

            for s in range(slots):
                got[s, :, c, q] = pick_piece(c, s)

    def last_send(s):
        @pl.loop(1, col_count)
        def _(d):
            send[last, other(d), s] = pick_piece(other(d), s)
            last_copy(s, d, c).start()

        got[s, :, c, last] = pick_piece(c, s)

    first = min(2, slots)

    @pl.loop(0, first)
    def _(s):
        last_send(s)

    @pl.loop(0, last)
    def _(q):
        arrived(send.at[q, 0 : col_count - 1], g_sems.at[q])

    for load in loads:
        load.wait()

    def back_copy(s, d, place):
        to = other(d)
        return remote(
            back.at[s, to],
            returned.at[place * slots + s],
            send_sems.at[7],
            back_sems.at[0],
            (t, to),
        )

    @pl.loop(0, slots)
    def _(s):
        arrived(send.at[last, 0 : col_count - 1, s], last_sems.at[s])

        @pl.when(s == 0)
        def _():
            @pl.loop(first, slots)
            def _(later):
                last_send(later)

        decay = jnp.where(table[s, 0, c] >= 0, f32(decay_rate), f32(1.0))
        result, left, right = slot_math(got[s].reshape(B, B), left_out[s], right_out[s], decay)
        back[s] = result.reshape(back.shape[1:])
        returned[c * slots + s] = back[s, c]
        left_out[s] = left
        right_out[s] = right
        for d in range(1, col_count):
            back_copy(s, d, c).start()

    def home_copy(d, place):
        to = other(d)
        return remote(
            leaving.at[to], home_ref.at[:, place], send_sems.at[8], home_sems.at[0], (t, to)
        )

    arrived(returned.at[0 : (col_count - 1) * slots], back_sems.at[0])
    block_width = width // per_home

    def fill(h, target):
        for p in range(per_home):
            piece_at = h * per_home + p
            for r in range(row_blocks):
                place = pick_ref[r * col_blocks + piece_at // per_block]
                block = returned[place]
                if per_block > 1:
                    part = lax.rem(piece_at, per_block)
                    parts = [block[:, k * width : (k + 1) * width] for k in range(per_block)]
                    block = parts[0]
                    for k in range(1, per_block):
                        block = jnp.where(part == k, parts[k], block)
                target[r, :, p * block_width : (p + 1) * block_width] = block

    @pl.loop(1, col_count)
    def _(d):
        fill(other(d), leaving.at[other(d)])
        home_copy(d, c).start()

    fill(c, home_ref.at[:, c])

    gone(act_buf.at[0 : tok_count - 1, 0, 0], send_sems.at[0])
    gone(act_buf.at[0 : tok_count - 1, 0 : chips - 1, 0], send_sems.at[1])
    gone(act_buf.at[0 : tok_count - 1, :, 0], send_sems.at[2])
    gone(og_turned.at[:, 0 : col_count - 1], send_sems.at[3])
    for k in range(tok_count - 1):

        @pl.when(t == k)
        def _():
            gone(og_buf.at[0 : k + 1], send_sems.at[4])

        @pl.when(tok_count - 1 - t == k)
        def _():
            gone(og_buf.at[0 : k + 1], send_sems.at[5])

    gone(send.at[:, 0 : col_count - 1], send_sems.at[6])
    gone(back.at[:, 0 : col_count - 1], send_sems.at[7])
    gone(leaving.at[0 : col_count - 1], send_sems.at[8])
    arrived(leaving.at[0 : col_count - 1], home_sems.at[0])


def place_kernel(in_ref, left_ref, right_ref, out_ref, left_out, right_out, sems):
    copies = [
        pltpu.make_async_copy(left_ref, left_out, sems.at[0]),
        pltpu.make_async_copy(right_ref, right_out, sems.at[1]),
        pltpu.make_async_copy(in_ref, out_ref, sems.at[2]),
    ]
    for copy in copies:
        copy.start()
    for copy in copies:
        copy.wait()


def per_device(activations, out_grad, owned_blocks, gram_left, gram_right):
    tok_count = lax.axis_size("tok")
    col_count = lax.axis_size("col")
    tok_local, shard_width = out_grad.shape
    rows_home = activations.shape[1] // tok_count
    row_blocks = rows_home // B
    col_blocks = shard_width * col_count // B
    piece_width = min(B, shard_width)
    per_home = shard_width // piece_width
    per_block = B // piece_width
    sub = piece_width // col_count
    chunks = max(1, sub // 16)
    rows_q = sub // chunks
    back_rows = B // col_count
    slots = owned_blocks.shape[2]
    smem = pl.BlockSpec(memory_space=pltpu.SMEM)

    act = activations.reshape(col_count // 2, 2, tok_local // col_count, activations.shape[1])
    sem = pltpu.SemaphoreType.DMA
    out, left_next, right_next = pl.pallas_call(
        functools.partial(main_kernel, slots),
        out_shape=[
            pltpu.VMEM((row_blocks, col_count, back_rows, shard_width), bf16),
            pltpu.VMEM((slots, B, B), f32),
            pltpu.VMEM((slots, B, B), f32),
        ],
        in_specs=[smem, ANY, ANY, ANY, ANY],
        out_specs=[VMEM, VMEM, VMEM],
        scratch_shapes=[
            pltpu.VMEM((tok_local, shard_width), bf16),
            pltpu.VMEM((per_home, col_count, chunks, rows_q, tok_local), bf16),
            pltpu.VMEM((tok_count, chunks, col_count, per_home, rows_q, tok_local), bf16),
            pltpu.VMEM(
                (tok_count, col_count // 2, 2, tok_local // col_count, rows_home), bf16
            ),
            pltpu.VMEM((row_blocks * col_blocks, per_block, rows_q, B), bf16),
            pltpu.VMEM((chunks, col_count, slots, per_block, rows_q, B), bf16),
            pltpu.VMEM((slots, per_block, col_count, chunks, rows_q, B), bf16),
            pltpu.VMEM((slots, col_count, back_rows, B), bf16),
            pltpu.VMEM((col_count * slots, back_rows, B), bf16),
            pltpu.VMEM((col_count, row_blocks, back_rows, shard_width), bf16),
            pltpu.SMEM((row_blocks * col_blocks,), jnp.int32),
            sem((9,)),
            sem((chunks,)),
            sem((tok_count,)),
            sem((tok_count,)),
            sem((tok_count,)),
            sem((chunks, tok_count)),
            sem((chunks,)),
            sem((slots,)),
            sem((1,)),
            sem((1,)),
            sem((4,)),
        ],
        compiler_params=pltpu.CompilerParams(
            collective_id=0, has_side_effects=True, vmem_limit_bytes=48 * MIB
        ),
    )(
        owned_blocks.transpose(2, 0, 1),
        *(
            pltpu.with_memory_space_constraint(x, pltpu.HBM)
            for x in (out_grad, act, gram_left[0, 0], gram_right[0, 0])
        ),
    )
    return tuple(
        pl.pallas_call(
            place_kernel,
            out_shape=[
                jax.ShapeDtypeStruct((rows_home, shard_width), bf16),
                jax.ShapeDtypeStruct((1, 1, slots, B, B), f32),
                jax.ShapeDtypeStruct((1, 1, slots, B, B), f32),
            ],
            in_specs=[VMEM, VMEM, VMEM],
            out_specs=[ANY, ANY, ANY],
            scratch_shapes=[pltpu.SemaphoreType.DMA((3,))],
            compiler_params=pltpu.CompilerParams(vmem_limit_bytes=16 * MIB),
        )(out.reshape(rows_home, shard_width), left_next[None, None], right_next[None, None])
    )


def solution(mesh):
    in_specs = (
        P("tok", None),
        P("tok", "col"),
        P("tok", None, None),
        P("tok", "col", None, None, None),
        P("tok", "col", None, None, None),
    )
    out_specs = (
        P("tok", "col"),
        P("tok", "col", None, None, None),
        P("tok", "col", None, None, None),
    )
    return jax.shard_map(
        per_device, mesh=mesh, in_specs=in_specs, out_specs=out_specs, check_vma=False
    )
```

```python
import functools

import jax
import jax.numpy as jnp
from jax import lax
from jax.experimental import pallas as pl
from jax.experimental.pallas import tpu as pltpu
from jax.sharding import PartitionSpec as P

B = 512
decay_rate = 0.9
epsilon = 1e-06
f32 = jnp.float32
bf16 = jnp.bfloat16
MESH = pl.DeviceIdType.MESH
VMEM = pl.BlockSpec(memory_space=pltpu.VMEM)
ANY = pl.BlockSpec(memory_space=pl.ANY)
MIB = 1024 * 1024


def mm(a, b):
    return jnp.dot(a.astype(bf16), b.astype(bf16), preferred_element_type=f32)


def root_minus_identity(matrix, diagonal):
    side = matrix.shape[-1]
    scale = 0.25 * side / jnp.sum(jnp.where(diagonal, matrix, 0.0))
    e = jnp.where(diagonal, 0.25, 0.0) - matrix * scale
    eb = e.astype(bf16)
    w = 2.0 * e + mm(eb, eb)
    v = w + e + mm(eb, w)
    r = v - 1.25 * w
    return (1.25 * e + r - 0.25 * v + mm(v, r)).astype(bf16)


def slot_math(gt, left_old, right_old, decay):
    g = gt.T
    rows = lax.broadcasted_iota(jnp.int32, (B, B), 0)
    cols = lax.broadcasted_iota(jnp.int32, (B, B), 1)
    diagonal = rows == cols
    left = decay * left_old + jnp.dot(g, gt, preferred_element_type=f32)
    right = decay * right_old + jnp.dot(gt, g, preferred_element_type=f32)
    yl = root_minus_identity(left, diagonal)
    yr = root_minus_identity(right, diagonal)
    g32 = g.astype(f32)
    first = g32 + jnp.dot(yl, g, preferred_element_type=f32)
    shaped = first + mm(first, yr)
    grad_norm = jnp.sqrt(jnp.sum(g32 * g32, keepdims=True) + epsilon)
    shaped_norm = jnp.sqrt(jnp.sum(shaped * shaped, keepdims=True) + epsilon)
    return (shaped * (grad_norm / shaped_norm)).astype(bf16), left, right


def main_kernel(
    slots,
    table,
    og_ref,
    act_ref,
    left_ref,
    right_ref,
    home_ref,
    left_out,
    right_out,
    og_in,
    og_turned,
    og_buf,
    act_buf,
    total,
    grad,
    send,
    got,
    back,
    returned_top,
    returned_low,
    leaving,
    pick_ref,
    send_sems,
    og_sems,
    act_sems,
    share_sems,
    partner_sems,
    z_sems,
    g_sems,
    last_sems,
    back_sems,
    home_sems,
    local_sems,
):
    t = lax.axis_index("tok")
    c = lax.axis_index("col")
    tok_count, chunks, col_count, per_home, rows_q, _ = og_buf.shape
    chips = col_count // 2
    core = lax.rem(c, 2)
    chip = c // 2
    partner = chip * 2 + 1 - core
    row_blocks, halves, width = home_ref.shape[0], home_ref.shape[1], home_ref.shape[4]
    col_blocks = grad.shape[0] // row_blocks
    per_block = got.shape[1]
    rows_home = act_buf.shape[4]
    base = t * (row_blocks * col_blocks)
    last = chunks - 1

    barrier = pltpu.get_barrier_semaphore()
    for d in range(1, col_count):
        pl.semaphore_signal(
            barrier, inc=1, device_id=(t, lax.rem(c + d, col_count)), device_id_type=MESH
        )
    for d in range(1, tok_count):
        pl.semaphore_signal(
            barrier, inc=1, device_id=(lax.rem(t + d, tok_count), c), device_id_type=MESH
        )

    def remote(src, dst, sent, received, to):
        return pltpu.make_async_remote_copy(
            src_ref=src,
            dst_ref=dst,
            send_sem=sent,
            recv_sem=received,
            device_id=to,
            device_id_type=MESH,
        )

    def arrived(size, sem):
        remote(size, size, sem, sem, (t, partner)).wait_recv()

    def gone(size, sem):
        remote(size, size, sem, sem, (t, partner)).wait_send()

    def other(d):
        return lax.rem(c + d, col_count)

    loads = [
        pltpu.make_async_copy(left_ref, left_out, local_sems.at[2]),
        pltpu.make_async_copy(right_ref, right_out, local_sems.at[3]),
    ]

    def act_columns(to):
        return pl.ds(pl.multiple_of(to * rows_home, rows_home), rows_home)

    og_load = pltpu.make_async_copy(og_ref, og_in, local_sems.at[0])
    og_load.start()
    own_act = pltpu.make_async_copy(
        act_ref.at[:, :, :, act_columns(t)], act_buf.at[t], local_sems.at[1]
    )
    own_act.start()
    for load in loads:
        load.start()

    og_load.wait()
    og_turned[...] = og_in[...].T.reshape(og_turned.shape)
    pl.semaphore_wait(barrier, col_count + tok_count - 2)

    def act_copy(source, d):
        to = lax.rem(source + d, tok_count)
        return remote(
            act_ref.at[chip, core, :, act_columns(to)],
            act_buf.at[source, chip, core],
            send_sems.at[0],
            act_sems.at[source],
            (to, c),
        )

    def act_wait(d):
        source = lax.rem(t + d, tok_count)
        piece = act_buf.at[source, chip, core]
        arrived(piece, act_sems.at[source])

    def share(d, m, held):
        token = lax.rem(t + d, tok_count)
        piece = act_buf.at[token, held, core]
        to = lax.rem(chip + m, chips) * 2 + core
        return remote(piece, piece, send_sems.at[1], share_sems.at[d], (t, to))

    def to_partner(d, lane):
        token = lax.rem(t + d, tok_count)
        half = act_buf.at[token, :, lane]
        return remote(half, half, send_sems.at[2], partner_sems.at[d], (t, partner))

    def og_copy(q, d, place):
        to = other(d)
        return remote(
            og_turned.at[:, to, q],
            og_buf.at[t, q, place],
            send_sems.at[3],
            og_sems.at[q],
            (t, to),
        )

    def along(origin, q, up):
        step = 1 if up else -1
        chunk = og_buf.at[origin, q]
        kind = 0 if up else 1
        return remote(
            chunk, chunk, send_sems.at[4 + kind], z_sems.at[q, origin], (t + step, c)
        )

    def og_start(q):
        og_buf[t, q, c] = og_turned[:, c, q]
        for d in range(1, col_count):
            og_copy(q, d, c).start()

    def og_on(q):
        arrived(og_turned.at[:, 0 : col_count - 1, q], og_sems.at[q])

        @pl.when(t < tok_count - 1)
        def _():
            along(t, q, True).start()

        @pl.when(t > 0)
        def _():
            along(t, q, False).start()

    def relay(q, then):
        @pl.loop(0, 2 * (tok_count - 1))
        def _(i):
            origin = t + (1 - 2 * lax.rem(i, 2)) * (i // 2 + 1)

            @pl.when((origin >= 0) & (origin < tok_count))
            def _():
                arrived(og_buf.at[origin, q], z_sems.at[q, origin])

                @pl.when((origin < t) & (t < tok_count - 1))
                def _():
                    along(origin, q, True).start()

                @pl.when((origin > t) & (t > 0))
                def _():
                    along(origin, q, False).start()

                then(origin)

    def product(q, k):
        rows = col_count * per_home * rows_q
        return jnp.dot(
            og_buf[k, q].reshape(rows, og_buf.shape[5]),
            act_buf[k].reshape(og_buf.shape[5], rows_home),
            preferred_element_type=f32,
        )

    def round_off():
        for r in range(row_blocks):
            piece = total[:, r * B : (r + 1) * B].reshape(col_blocks, per_block, rows_q, B)
            grad[pl.ds(r * col_blocks, col_blocks)] = piece.astype(bf16)

    def pick_piece(o, s):
        owned = table[s, 0, o]
        piece = grad[jnp.maximum(owned - base, 0)]
        return jnp.where(owned >= 0, piece, jnp.zeros_like(piece))

    def g_copy(q, d, place):
        to = other(d)
        return remote(
            send.at[q, to],
            got.at[:, :, place, q],
            send_sems.at[6],
            g_sems.at[q],
            (t, to),
        )

    def last_copy(s, d, place):
        to = other(d)
        return remote(
            send.at[last, to, s],
            got.at[s, :, place, last],
            send_sems.at[6],
            last_sems.at[s],
            (t, to),
        )

    edge = (t == 0) | (t == tok_count - 1)
    early = min(2, chunks)
    og_start(0)
    for d in range(1, tok_count):
        act_copy(t, d).start()
    for q in range(1, chunks):
        og_start(q)
    for q in range(early):
        og_on(q)

    for d in range(1, tok_count):
        act_wait(d)
        for m in range(1, chips):
            share(d, m, chip).start()

    @pl.when(edge)
    def _():
        for q in range(early, chunks):
            og_on(q)

    @pl.loop(0, row_blocks * col_blocks)
    def _(place):
        found = jnp.int32(0)
        for s in range(slots):
            for o in range(col_count):
                found = jnp.where(table[s, 0, o] == base + place, o * slots + s, found)
        pick_ref[place] = found

    def add(q, k):
        total[...] += product(q, k)

    @pl.loop(0, chunks)
    def _(q):
        @pl.when(q > 0)
        def _():
            total[...] = product(q, t)

        relay(q, lambda origin: pl.when(q > 0)(lambda: add(q, origin)))

        @pl.when(q == 0)
        def _():
            for d in range(1, tok_count):
                arrived(act_buf.at[0, 0 : chips - 1, 0], share_sems.at[d])
                to_partner(d, core).start()

        @pl.when(jnp.logical_not(edge) & (q + early < chunks))
        def _():
            og_on(q + early)

        @pl.when(q == 0)
        def _():
            own_act.wait()
            total[...] = product(q, t)
            for d in range(1, tok_count):
                to_partner(d, 1 - core).wait_recv()

            @pl.loop(1, tok_count)
            def _(d):
                add(q, lax.rem(t + d, tok_count))

        round_off()

        @pl.when(q < last)
        def _():
            @pl.loop(1, col_count)
            def _(d):
                for s in range(slots):
                    send[q, other(d), s] = pick_piece(other(d), s)
                g_copy(q, d, c).start()

            for s in range(slots):
                got[s, :, c, q] = pick_piece(c, s)

    def last_send(s):
        @pl.loop(1, col_count)
        def _(d):
            send[last, other(d), s] = pick_piece(other(d), s)
            last_copy(s, d, c).start()

        got[s, :, c, last] = pick_piece(c, s)

    first = min(2, slots)

    @pl.loop(0, first)
    def _(s):
        last_send(s)

    @pl.loop(0, last)
    def _(q):
        arrived(send.at[q, 0 : col_count - 1], g_sems.at[q])

    for load in loads:
        load.wait()

    returned = (returned_top, returned_low)

    def back_start(half, s):
        for d in range(1, col_count):
            to = other(d)
            remote(
                back.at[half, s, to],
                returned[half].at[c * slots + s],
                send_sems.at[7],
                back_sems.at[half],
                (t, to),
            ).start()

    held = max(slots - 2, 0)

    @pl.loop(0, slots)
    def _(s):
        arrived(send.at[last, 0 : col_count - 1, s], last_sems.at[s])

        @pl.when(s == 0)
        def _():
            @pl.loop(first, slots)
            def _(later):
                last_send(later)

        decay = jnp.where(table[s, 0, c] >= 0, f32(decay_rate), f32(1.0))
        result, left, right = slot_math(got[s].reshape(B, B), left_out[s], right_out[s], decay)
        for half in range(halves):
            rows = slice(half * (B // halves), (half + 1) * (B // halves))
            back[half, s] = result[rows].reshape(back.shape[2:])
            returned[half][c * slots + s] = back[half, s, c]
        left_out[s] = left
        right_out[s] = right
        back_start(0, s)
        for half in range(1, halves):

            @pl.when(s < held)
            def _():
                back_start(half, s)

    for half in range(1, halves):

        @pl.loop(held, slots)
        def _(s):
            back_start(half, s)

    block_width = width // per_home

    def fill(half, h, target):
        for p in range(per_home):
            piece_at = h * per_home + p
            for r in range(row_blocks):
                place = pick_ref[r * col_blocks + piece_at // per_block]
                block = returned[half][place]
                if per_block > 1:
                    part = lax.rem(piece_at, per_block)
                    parts = [block[:, k * width : (k + 1) * width] for k in range(per_block)]
                    block = parts[0]
                    for k in range(1, per_block):
                        block = jnp.where(part == k, parts[k], block)
                target[r, :, p * block_width : (p + 1) * block_width] = block

    for half in range(halves):
        arrived(returned[half].at[0 : (col_count - 1) * slots], back_sems.at[half])

        @pl.loop(1, col_count)
        def _(d):
            to = other(d)
            fill(half, to, leaving.at[half, to])
            remote(
                leaving.at[half, to],
                home_ref.at[:, half, c],
                send_sems.at[8],
                home_sems.at[0],
                (t, to),
            ).start()

        fill(half, c, home_ref.at[:, half, c])

    gone(act_buf.at[0 : tok_count - 1, 0, 0], send_sems.at[0])
    gone(act_buf.at[0 : tok_count - 1, 0 : chips - 1, 0], send_sems.at[1])
    gone(act_buf.at[0 : tok_count - 1, :, 0], send_sems.at[2])
    gone(og_turned.at[:, 0 : col_count - 1], send_sems.at[3])
    for k in range(tok_count - 1):

        @pl.when(t == k)
        def _():
            gone(og_buf.at[0 : k + 1], send_sems.at[4])

        @pl.when(tok_count - 1 - t == k)
        def _():
            gone(og_buf.at[0 : k + 1], send_sems.at[5])

    gone(send.at[:, 0 : col_count - 1], send_sems.at[6])
    gone(back.at[:, :, 0 : col_count - 1], send_sems.at[7])
    gone(leaving.at[:, 0 : col_count - 1], send_sems.at[8])
    arrived(leaving.at[:, 0 : col_count - 1], home_sems.at[0])


def place_kernel(in_ref, left_ref, right_ref, out_ref, left_out, right_out, sems):
    slots = left_ref.shape[2]
    copies = [pltpu.make_async_copy(in_ref, out_ref, sems.at[0])]
    for s in range(slots):
        for k, (source, target) in enumerate(((left_ref, left_out), (right_ref, right_out))):
            copies.append(
                pltpu.make_async_copy(
                    source.at[0, 0, s], target.at[0, 0, s], sems.at[1 + 2 * s + k]
                )
            )
    for copy in copies:
        copy.start()
    for copy in copies:
        copy.wait()


def per_device(activations, out_grad, owned_blocks, gram_left, gram_right):
    tok_count = lax.axis_size("tok")
    col_count = lax.axis_size("col")
    tok_local, shard_width = out_grad.shape
    rows_home = activations.shape[1] // tok_count
    row_blocks = rows_home // B
    col_blocks = shard_width * col_count // B
    piece_width = min(B, shard_width)
    per_home = shard_width // piece_width
    per_block = B // piece_width
    sub = piece_width // col_count
    chunks = max(1, sub // 16)
    rows_q = sub // chunks
    halves = max(1, min(2, B // col_count // 16))
    back_rows = B // col_count // halves
    slots = owned_blocks.shape[2]
    smem = pl.BlockSpec(memory_space=pltpu.SMEM)

    act = activations.reshape(col_count // 2, 2, tok_local // col_count, activations.shape[1])
    sem = pltpu.SemaphoreType.DMA
    out, left_next, right_next = pl.pallas_call(
        functools.partial(main_kernel, slots),
        out_shape=[
            pltpu.VMEM((row_blocks, halves, col_count, back_rows, shard_width), bf16),
            pltpu.VMEM((slots, B, B), f32),
            pltpu.VMEM((slots, B, B), f32),
        ],
        in_specs=[smem, ANY, ANY, ANY, ANY],
        out_specs=[VMEM, VMEM, VMEM],
        scratch_shapes=[
            pltpu.VMEM((tok_local, shard_width), bf16),
            pltpu.VMEM((per_home, col_count, chunks, rows_q, tok_local), bf16),
            pltpu.VMEM((tok_count, chunks, col_count, per_home, rows_q, tok_local), bf16),
            pltpu.VMEM(
                (tok_count, col_count // 2, 2, tok_local // col_count, rows_home), bf16
            ),
            pltpu.VMEM((col_count * per_home * rows_q, rows_home), f32),
            pltpu.VMEM((row_blocks * col_blocks, per_block, rows_q, B), bf16),
            pltpu.VMEM((chunks, col_count, slots, per_block, rows_q, B), bf16),
            pltpu.VMEM((slots, per_block, col_count, chunks, rows_q, B), bf16),
            pltpu.VMEM((halves, slots, col_count, back_rows, B), bf16),
            pltpu.VMEM((col_count * slots, back_rows, B), bf16),
            pltpu.VMEM((col_count * slots, back_rows, B), bf16),
            pltpu.VMEM((halves, col_count, row_blocks, back_rows, shard_width), bf16),
            pltpu.SMEM((row_blocks * col_blocks,), jnp.int32),
            sem((9,)),
            sem((chunks,)),
            sem((tok_count,)),
            sem((tok_count,)),
            sem((tok_count,)),
            sem((chunks, tok_count)),
            sem((chunks,)),
            sem((slots,)),
            sem((halves,)),
            sem((1,)),
            sem((4,)),
        ],
        compiler_params=pltpu.CompilerParams(
            collective_id=0, has_side_effects=True, vmem_limit_bytes=48 * MIB
        ),
    )(
        owned_blocks.transpose(2, 0, 1),
        *(
            pltpu.with_memory_space_constraint(x, pltpu.HBM)
            for x in (out_grad, act, gram_left[0, 0], gram_right[0, 0])
        ),
    )
    return tuple(
        pl.pallas_call(
            place_kernel,
            out_shape=[
                jax.ShapeDtypeStruct((rows_home, shard_width), bf16),
                jax.ShapeDtypeStruct((1, 1, slots, B, B), f32),
                jax.ShapeDtypeStruct((1, 1, slots, B, B), f32),
            ],
            in_specs=[VMEM, VMEM, VMEM],
            out_specs=[ANY, ANY, ANY],
            scratch_shapes=[pltpu.SemaphoreType.DMA((1 + 2 * slots,))],
            compiler_params=pltpu.CompilerParams(vmem_limit_bytes=16 * MIB),
        )(out.reshape(rows_home, shard_width), left_next[None, None], right_next[None, None])
    )


def solution(mesh):
    in_specs = (
        P("tok", None),
        P("tok", "col"),
        P("tok", None, None),
        P("tok", "col", None, None, None),
        P("tok", "col", None, None, None),
    )
    out_specs = (
        P("tok", "col"),
        P("tok", "col", None, None, None),
        P("tok", "col", None, None, None),
    )
    return jax.shard_map(
        per_device, mesh=mesh, in_specs=in_specs, out_specs=out_specs, check_vma=False
    )
```

```python
import functools

import jax
import jax.numpy as jnp
from jax import lax
from jax.experimental import pallas as pl
from jax.experimental.pallas import tpu as pltpu
from jax.sharding import PartitionSpec as P

B = 512
decay_rate = 0.9
epsilon = 1e-06
f32 = jnp.float32
bf16 = jnp.bfloat16
MESH = pl.DeviceIdType.MESH
VMEM = pl.BlockSpec(memory_space=pltpu.VMEM)
ANY = pl.BlockSpec(memory_space=pl.ANY)
MIB = 1024 * 1024


def mm(a, b):
    return jnp.dot(a.astype(bf16), b.astype(bf16), preferred_element_type=f32)


def root_minus_identity(matrix, diagonal):
    side = matrix.shape[-1]
    scale = 0.25 * side / jnp.sum(jnp.where(diagonal, matrix, 0.0))
    e = jnp.where(diagonal, 0.25, 0.0) - matrix * scale
    eb = e.astype(bf16)
    w = 2.0 * e + mm(eb, eb)
    v = w + e + mm(eb, w)
    r = v - 1.25 * w
    return (1.25 * e + r - 0.25 * v + mm(v, r)).astype(bf16)


def slot_math(gt, left_old, right_old, decay):
    g = gt.T
    rows = lax.broadcasted_iota(jnp.int32, (B, B), 0)
    cols = lax.broadcasted_iota(jnp.int32, (B, B), 1)
    diagonal = rows == cols
    left = decay * left_old + jnp.dot(g, gt, preferred_element_type=f32)
    right = decay * right_old + jnp.dot(gt, g, preferred_element_type=f32)
    yl = root_minus_identity(left, diagonal)
    yr = root_minus_identity(right, diagonal)
    g32 = g.astype(f32)
    first = g32 + jnp.dot(yl, g, preferred_element_type=f32)
    shaped = first + mm(first, yr)
    grad_norm = jnp.sqrt(jnp.sum(g32 * g32, keepdims=True) + epsilon)
    shaped_norm = jnp.sqrt(jnp.sum(shaped * shaped, keepdims=True) + epsilon)
    return (shaped * (grad_norm / shaped_norm)).astype(bf16), left, right


def main_kernel(
    slots,
    table,
    og_ref,
    act_ref,
    left_ref,
    right_ref,
    home_ref,
    left_out,
    right_out,
    og_in,
    og_turned,
    og_buf,
    act_buf,
    total,
    grad,
    send,
    got,
    back,
    returned_top,
    returned_low,
    leaving,
    pick_ref,
    send_sems,
    og_sems,
    act_sems,
    share_sems,
    partner_sems,
    z_sems,
    g_sems,
    last_sems,
    back_sems,
    home_sems,
    local_sems,
):
    t = lax.axis_index("tok")
    c = lax.axis_index("col")
    tok_count, chunks, col_count, per_home, rows_q, _ = og_buf.shape
    chips = col_count // 2
    core = lax.rem(c, 2)
    chip = c // 2
    partner = chip * 2 + 1 - core
    row_blocks, halves, width = home_ref.shape[0], home_ref.shape[1], home_ref.shape[4]
    col_blocks = grad.shape[0] // row_blocks
    per_block = got.shape[1]
    rows_home = act_buf.shape[4]
    base = t * (row_blocks * col_blocks)
    last = chunks - 1

    barrier = pltpu.get_barrier_semaphore()
    for d in range(1, col_count):
        pl.semaphore_signal(
            barrier, inc=1, device_id=(t, lax.rem(c + d, col_count)), device_id_type=MESH
        )
    for d in range(1, tok_count):
        pl.semaphore_signal(
            barrier, inc=1, device_id=(lax.rem(t + d, tok_count), c), device_id_type=MESH
        )

    def remote(src, dst, sent, received, to):
        return pltpu.make_async_remote_copy(
            src_ref=src,
            dst_ref=dst,
            send_sem=sent,
            recv_sem=received,
            device_id=to,
            device_id_type=MESH,
        )

    def arrived(size, sem):
        remote(size, size, sem, sem, (t, partner)).wait_recv()

    def gone(size, sem):
        remote(size, size, sem, sem, (t, partner)).wait_send()

    def other(d):
        return lax.rem(c + d, col_count)

    loads = [
        pltpu.make_async_copy(left_ref, left_out, local_sems.at[2]),
        pltpu.make_async_copy(right_ref, right_out, local_sems.at[3]),
    ]

    def act_columns(to):
        return pl.ds(pl.multiple_of(to * rows_home, rows_home), rows_home)

    og_load = pltpu.make_async_copy(og_ref, og_in, local_sems.at[0])
    og_load.start()
    own_act = pltpu.make_async_copy(
        act_ref.at[:, :, :, act_columns(t)], act_buf.at[t], local_sems.at[1]
    )
    own_act.start()
    for load in loads:
        load.start()

    og_load.wait()
    og_turned[...] = og_in[...].T.reshape(og_turned.shape)
    pl.semaphore_wait(barrier, col_count + tok_count - 2)

    def act_copy(source, d):
        to = lax.rem(source + d, tok_count)
        return remote(
            act_ref.at[chip, core, :, act_columns(to)],
            act_buf.at[source, chip, core],
            send_sems.at[0],
            act_sems.at[source],
            (to, c),
        )

    def act_wait(d):
        source = lax.rem(t + d, tok_count)
        piece = act_buf.at[source, chip, core]
        arrived(piece, act_sems.at[source])

    def share(d, m, held):
        token = lax.rem(t + d, tok_count)
        piece = act_buf.at[token, held, core]
        to = lax.rem(chip + m, chips) * 2 + core
        return remote(piece, piece, send_sems.at[1], share_sems.at[d], (t, to))

    def to_partner(d, lane):
        token = lax.rem(t + d, tok_count)
        half = act_buf.at[token, :, lane]
        return remote(half, half, send_sems.at[2], partner_sems.at[d], (t, partner))

    def og_copy(q, d, place):
        to = other(d)
        return remote(
            og_turned.at[:, to, q],
            og_buf.at[t, q, place],
            send_sems.at[3],
            og_sems.at[q],
            (t, to),
        )

    def along(origin, q, up):
        step = 1 if up else -1
        chunk = og_buf.at[origin, q]
        kind = 0 if up else 1
        return remote(
            chunk, chunk, send_sems.at[4 + kind], z_sems.at[q, origin], (t + step, c)
        )

    def og_start(q):
        og_buf[t, q, c] = og_turned[:, c, q]
        for d in range(1, col_count):
            og_copy(q, d, c).start()

    def og_on(q):
        arrived(og_turned.at[:, 0 : col_count - 1, q], og_sems.at[q])

        @pl.when(t < tok_count - 1)
        def _():
            along(t, q, True).start()

        @pl.when(t > 0)
        def _():
            along(t, q, False).start()

    def relay(q):
        @pl.loop(0, 2 * (tok_count - 1))
        def _(i):
            origin = t + (1 - 2 * lax.rem(i, 2)) * (i // 2 + 1)

            @pl.when((origin >= 0) & (origin < tok_count))
            def _():
                arrived(og_buf.at[origin, q], z_sems.at[q, origin])

                @pl.when((origin < t) & (t < tok_count - 1))
                def _():
                    along(origin, q, True).start()

                @pl.when((origin > t) & (t > 0))
                def _():
                    along(origin, q, False).start()

    def product(q, k):
        rows = col_count * per_home * rows_q
        return jnp.dot(
            og_buf[k, q].reshape(rows, og_buf.shape[5]),
            act_buf[k].reshape(og_buf.shape[5], rows_home),
            preferred_element_type=f32,
        )

    def round_off():
        for r in range(row_blocks):
            piece = total[:, r * B : (r + 1) * B].reshape(col_blocks, per_block, rows_q, B)
            grad[pl.ds(r * col_blocks, col_blocks)] = piece.astype(bf16)

    def pick_piece(o, s):
        owned = table[s, 0, o]
        piece = grad[jnp.maximum(owned - base, 0)]
        return jnp.where(owned >= 0, piece, jnp.zeros_like(piece))

    def g_copy(q, d, place):
        to = other(d)
        return remote(
            send.at[q, to],
            got.at[:, :, place, q],
            send_sems.at[6],
            g_sems.at[q],
            (t, to),
        )

    def last_copy(s, d, place):
        to = other(d)
        return remote(
            send.at[last, to, s],
            got.at[s, :, place, last],
            send_sems.at[6],
            last_sems.at[s],
            (t, to),
        )

    edge = (t == 0) | (t == tok_count - 1)
    early = min(2, chunks)
    og_start(0)
    for d in range(1, tok_count):
        act_copy(t, d).start()
    for q in range(1, chunks):
        og_start(q)
    for q in range(early):
        og_on(q)

    for d in range(1, tok_count):
        act_wait(d)
        for m in range(1, chips):
            share(d, m, chip).start()

    @pl.when(edge)
    def _():
        for q in range(early, chunks):
            og_on(q)

    @pl.loop(0, row_blocks * col_blocks)
    def _(place):
        found = jnp.int32(0)
        for s in range(slots):
            for o in range(col_count):
                found = jnp.where(table[s, 0, o] == base + place, o * slots + s, found)
        pick_ref[place] = found

    @pl.loop(0, chunks)
    def _(q):
        @pl.when(edge | (q == 0))
        def _():
            relay(q)

        @pl.when(q == 0)
        def _():
            for d in range(1, tok_count):
                arrived(act_buf.at[0, 0 : chips - 1, 0], share_sems.at[d])
                to_partner(d, core).start()

        @pl.when(jnp.logical_not(edge))
        def _():
            @pl.when(q + early < chunks)
            def _():
                og_on(q + early)

            @pl.when(q + 1 < chunks)
            def _():
                relay(q + 1)

        @pl.when(q == 0)
        def _():
            own_act.wait()
            for d in range(1, tok_count):
                to_partner(d, 1 - core).wait_recv()

        total[...] = sum(product(q, k) for k in range(tok_count))

        round_off()

        @pl.when(q < last)
        def _():
            @pl.loop(1, col_count)
            def _(d):
                for s in range(slots):
                    send[q, other(d), s] = pick_piece(other(d), s)
                g_copy(q, d, c).start()

            for s in range(slots):
                got[s, :, c, q] = pick_piece(c, s)

    def last_send(s):
        @pl.loop(1, col_count)
        def _(d):
            send[last, other(d), s] = pick_piece(other(d), s)
            last_copy(s, d, c).start()

        got[s, :, c, last] = pick_piece(c, s)

    first = min(2, slots)

    @pl.loop(0, first)
    def _(s):
        last_send(s)

    @pl.loop(0, last)
    def _(q):
        arrived(send.at[q, 0 : col_count - 1], g_sems.at[q])

    for load in loads:
        load.wait()

    returned = (returned_top, returned_low)

    def back_start(half, s):
        for d in range(1, col_count):
            to = other(d)
            remote(
                back.at[half, s, to],
                returned[half].at[c * slots + s],
                send_sems.at[7],
                back_sems.at[half],
                (t, to),
            ).start()

    held = max(slots - 1, 0)

    @pl.loop(0, slots)
    def _(s):
        arrived(send.at[last, 0 : col_count - 1, s], last_sems.at[s])

        @pl.when(s == 0)
        def _():
            @pl.loop(first, slots)
            def _(later):
                last_send(later)

        decay = jnp.where(table[s, 0, c] >= 0, f32(decay_rate), f32(1.0))
        result, left, right = slot_math(got[s].reshape(B, B), left_out[s], right_out[s], decay)
        for half in range(halves):
            rows = slice(half * (B // halves), (half + 1) * (B // halves))
            back[half, s] = result[rows].reshape(back.shape[2:])
            returned[half][c * slots + s] = back[half, s, c]
        left_out[s] = left
        right_out[s] = right
        back_start(0, s)
        for half in range(1, halves):

            @pl.when(s < held)
            def _():
                back_start(half, s)

    for half in range(1, halves):

        @pl.loop(held, slots)
        def _(s):
            back_start(half, s)

    block_width = width // per_home

    def fill(half, h, target):
        for p in range(per_home):
            piece_at = h * per_home + p
            for r in range(row_blocks):
                place = pick_ref[r * col_blocks + piece_at // per_block]
                block = returned[half][place]
                if per_block > 1:
                    part = lax.rem(piece_at, per_block)
                    parts = [block[:, k * width : (k + 1) * width] for k in range(per_block)]
                    block = parts[0]
                    for k in range(1, per_block):
                        block = jnp.where(part == k, parts[k], block)
                target[r, :, p * block_width : (p + 1) * block_width] = block

    for half in range(halves):
        arrived(returned[half].at[0 : (col_count - 1) * slots], back_sems.at[half])

        @pl.loop(1, col_count)
        def _(d):
            to = other(d)
            fill(half, to, leaving.at[half, to])
            remote(
                leaving.at[half, to],
                home_ref.at[:, half, c],
                send_sems.at[8],
                home_sems.at[0],
                (t, to),
            ).start()

        fill(half, c, home_ref.at[:, half, c])

    gone(act_buf.at[0 : tok_count - 1, 0, 0], send_sems.at[0])
    gone(act_buf.at[0 : tok_count - 1, 0 : chips - 1, 0], send_sems.at[1])
    gone(act_buf.at[0 : tok_count - 1, :, 0], send_sems.at[2])
    gone(og_turned.at[:, 0 : col_count - 1], send_sems.at[3])
    for k in range(tok_count - 1):

        @pl.when(t == k)
        def _():
            gone(og_buf.at[0 : k + 1], send_sems.at[4])

        @pl.when(tok_count - 1 - t == k)
        def _():
            gone(og_buf.at[0 : k + 1], send_sems.at[5])

    gone(send.at[:, 0 : col_count - 1], send_sems.at[6])
    gone(back.at[:, :, 0 : col_count - 1], send_sems.at[7])
    gone(leaving.at[:, 0 : col_count - 1], send_sems.at[8])
    arrived(leaving.at[:, 0 : col_count - 1], home_sems.at[0])


def place_kernel(in_ref, left_ref, right_ref, out_ref, left_out, right_out, sems):
    slots = left_ref.shape[2]
    copies = [pltpu.make_async_copy(in_ref, out_ref, sems.at[0])]
    for s in range(slots):
        for k, (source, target) in enumerate(((left_ref, left_out), (right_ref, right_out))):
            copies.append(
                pltpu.make_async_copy(
                    source.at[0, 0, s], target.at[0, 0, s], sems.at[1 + 2 * s + k]
                )
            )
    for copy in copies:
        copy.start()
    for copy in copies:
        copy.wait()


def per_device(activations, out_grad, owned_blocks, gram_left, gram_right):
    tok_count = lax.axis_size("tok")
    col_count = lax.axis_size("col")
    tok_local, shard_width = out_grad.shape
    rows_home = activations.shape[1] // tok_count
    row_blocks = rows_home // B
    col_blocks = shard_width * col_count // B
    piece_width = min(B, shard_width)
    per_home = shard_width // piece_width
    per_block = B // piece_width
    sub = piece_width // col_count
    chunks = max(1, sub // 16)
    rows_q = sub // chunks
    halves = max(1, min(2, B // col_count // 16))
    back_rows = B // col_count // halves
    slots = owned_blocks.shape[2]
    smem = pl.BlockSpec(memory_space=pltpu.SMEM)

    act = activations.reshape(col_count // 2, 2, tok_local // col_count, activations.shape[1])
    sem = pltpu.SemaphoreType.DMA
    out, left_next, right_next = pl.pallas_call(
        functools.partial(main_kernel, slots),
        out_shape=[
            pltpu.VMEM((row_blocks, halves, col_count, back_rows, shard_width), bf16),
            pltpu.VMEM((slots, B, B), f32),
            pltpu.VMEM((slots, B, B), f32),
        ],
        in_specs=[smem, ANY, ANY, ANY, ANY],
        out_specs=[VMEM, VMEM, VMEM],
        scratch_shapes=[
            pltpu.VMEM((tok_local, shard_width), bf16),
            pltpu.VMEM((per_home, col_count, chunks, rows_q, tok_local), bf16),
            pltpu.VMEM((tok_count, chunks, col_count, per_home, rows_q, tok_local), bf16),
            pltpu.VMEM(
                (tok_count, col_count // 2, 2, tok_local // col_count, rows_home), bf16
            ),
            pltpu.VMEM((col_count * per_home * rows_q, rows_home), f32),
            pltpu.VMEM((row_blocks * col_blocks, per_block, rows_q, B), bf16),
            pltpu.VMEM((chunks, col_count, slots, per_block, rows_q, B), bf16),
            pltpu.VMEM((slots, per_block, col_count, chunks, rows_q, B), bf16),
            pltpu.VMEM((halves, slots, col_count, back_rows, B), bf16),
            pltpu.VMEM((col_count * slots, back_rows, B), bf16),
            pltpu.VMEM((col_count * slots, back_rows, B), bf16),
            pltpu.VMEM((halves, col_count, row_blocks, back_rows, shard_width), bf16),
            pltpu.SMEM((row_blocks * col_blocks,), jnp.int32),
            sem((9,)),
            sem((chunks,)),
            sem((tok_count,)),
            sem((tok_count,)),
            sem((tok_count,)),
            sem((chunks, tok_count)),
            sem((chunks,)),
            sem((slots,)),
            sem((halves,)),
            sem((1,)),
            sem((4,)),
        ],
        compiler_params=pltpu.CompilerParams(
            collective_id=0, has_side_effects=True, vmem_limit_bytes=48 * MIB
        ),
    )(
        owned_blocks.transpose(2, 0, 1),
        *(
            pltpu.with_memory_space_constraint(x, pltpu.HBM)
            for x in (out_grad, act, gram_left[0, 0], gram_right[0, 0])
        ),
    )
    return tuple(
        pl.pallas_call(
            place_kernel,
            out_shape=[
                jax.ShapeDtypeStruct((rows_home, shard_width), bf16),
                jax.ShapeDtypeStruct((1, 1, slots, B, B), f32),
                jax.ShapeDtypeStruct((1, 1, slots, B, B), f32),
            ],
            in_specs=[VMEM, VMEM, VMEM],
            out_specs=[ANY, ANY, ANY],
            scratch_shapes=[pltpu.SemaphoreType.DMA((1 + 2 * slots,))],
            compiler_params=pltpu.CompilerParams(vmem_limit_bytes=16 * MIB),
        )(out.reshape(rows_home, shard_width), left_next[None, None], right_next[None, None])
    )


def solution(mesh):
    in_specs = (
        P("tok", None),
        P("tok", "col"),
        P("tok", None, None),
        P("tok", "col", None, None, None),
        P("tok", "col", None, None, None),
    )
    out_specs = (
        P("tok", "col"),
        P("tok", "col", None, None, None),
        P("tok", "col", None, None, None),
    )
    return jax.shard_map(
        per_device, mesh=mesh, in_specs=in_specs, out_specs=out_specs, check_vma=False
    )
```

```python
import functools

import jax
import jax.numpy as jnp
from jax import lax
from jax.experimental import pallas as pl
from jax.experimental.pallas import tpu as pltpu
from jax.sharding import PartitionSpec as P

B = 512
decay_rate = 0.9
epsilon = 1e-06
f32 = jnp.float32
bf16 = jnp.bfloat16
MESH = pl.DeviceIdType.MESH
VMEM = pl.BlockSpec(memory_space=pltpu.VMEM)
ANY = pl.BlockSpec(memory_space=pl.ANY)
MIB = 1024 * 1024


def mm(a, b):
    return jnp.dot(a.astype(bf16), b.astype(bf16), preferred_element_type=f32)


def root_minus_identity(matrix, diagonal):
    side = matrix.shape[-1]
    scale = 0.25 * side / jnp.sum(jnp.where(diagonal, matrix, 0.0))
    e = jnp.where(diagonal, 0.25, 0.0) - matrix * scale
    eb = e.astype(bf16)
    w = 2.0 * e + mm(eb, eb)
    v = w + e + mm(eb, w)
    r = v - 1.25 * w
    return (1.25 * e + r - 0.25 * v + mm(v, r)).astype(bf16)


def slot_math(gt, left_old, right_old, decay):
    g = gt.T
    rows = lax.broadcasted_iota(jnp.int32, (B, B), 0)
    cols = lax.broadcasted_iota(jnp.int32, (B, B), 1)
    diagonal = rows == cols
    left = decay * left_old + jnp.dot(g, gt, preferred_element_type=f32)
    right = decay * right_old + jnp.dot(gt, g, preferred_element_type=f32)
    yl = root_minus_identity(left, diagonal)
    yr = root_minus_identity(right, diagonal)
    g32 = g.astype(f32)
    first = g32 + jnp.dot(yl, g, preferred_element_type=f32)
    shaped = first + mm(first, yr)
    grad_norm = jnp.sqrt(jnp.sum(g32 * g32, keepdims=True) + epsilon)
    shaped_norm = jnp.sqrt(jnp.sum(shaped * shaped, keepdims=True) + epsilon)
    return (shaped * (grad_norm / shaped_norm)).astype(bf16), left, right


def main_kernel(
    slots,
    table,
    og_ref,
    act_ref,
    left_ref,
    right_ref,
    home_ref,
    left_out,
    right_out,
    og_in,
    og_turned,
    og_buf,
    act_buf,
    total,
    grad,
    send,
    got,
    back,
    returned_top,
    returned_low,
    leaving,
    pick_ref,
    send_sems,
    og_sems,
    act_sems,
    share_sems,
    partner_sems,
    z_sems,
    g_sems,
    last_sems,
    back_sems,
    home_sems,
    local_sems,
):
    t = lax.axis_index("tok")
    c = lax.axis_index("col")
    tok_count, chunks, col_count, per_home, rows_q, _ = og_buf.shape
    chips = col_count // 2
    core = lax.rem(c, 2)
    chip = c // 2
    partner = chip * 2 + 1 - core
    row_blocks, halves, width = home_ref.shape[0], home_ref.shape[1], home_ref.shape[4]
    col_blocks = grad.shape[0] // row_blocks
    per_block = got.shape[1]
    rows_home = act_buf.shape[4]
    base = t * (row_blocks * col_blocks)
    last = chunks - 1

    barrier = pltpu.get_barrier_semaphore()
    for d in range(1, col_count):
        pl.semaphore_signal(
            barrier, inc=1, device_id=(t, lax.rem(c + d, col_count)), device_id_type=MESH
        )
    for d in range(1, tok_count):
        pl.semaphore_signal(
            barrier, inc=1, device_id=(lax.rem(t + d, tok_count), c), device_id_type=MESH
        )

    def remote(src, dst, sent, received, to):
        return pltpu.make_async_remote_copy(
            src_ref=src,
            dst_ref=dst,
            send_sem=sent,
            recv_sem=received,
            device_id=to,
            device_id_type=MESH,
        )

    def arrived(size, sem):
        remote(size, size, sem, sem, (t, partner)).wait_recv()

    def gone(size, sem):
        remote(size, size, sem, sem, (t, partner)).wait_send()

    def other(d):
        return lax.rem(c + d, col_count)

    loads = [
        pltpu.make_async_copy(left_ref, left_out, local_sems.at[2]),
        pltpu.make_async_copy(right_ref, right_out, local_sems.at[3]),
    ]

    def act_columns(to):
        return pl.ds(pl.multiple_of(to * rows_home, rows_home), rows_home)

    og_load = pltpu.make_async_copy(og_ref, og_in, local_sems.at[0])
    og_load.start()
    own_act = pltpu.make_async_copy(
        act_ref.at[:, :, :, act_columns(t)], act_buf.at[t], local_sems.at[1]
    )
    own_act.start()
    for load in loads:
        load.start()

    og_load.wait()
    og_turned[...] = og_in[...].T.reshape(og_turned.shape)
    pl.semaphore_wait(barrier, col_count + tok_count - 2)

    def act_copy(source, d):
        to = lax.rem(source + d, tok_count)
        return remote(
            act_ref.at[chip, core, :, act_columns(to)],
            act_buf.at[source, chip, core],
            send_sems.at[0],
            act_sems.at[source],
            (to, c),
        )

    def act_wait(d):
        source = lax.rem(t + d, tok_count)
        piece = act_buf.at[source, chip, core]
        arrived(piece, act_sems.at[source])

    def share(d, m, held):
        token = lax.rem(t + d, tok_count)
        piece = act_buf.at[token, held, core]
        to = lax.rem(chip + m, chips) * 2 + core
        return remote(piece, piece, send_sems.at[1], share_sems.at[d], (t, to))

    def to_partner(d, lane):
        token = lax.rem(t + d, tok_count)
        half = act_buf.at[token, :, lane]
        return remote(half, half, send_sems.at[2], partner_sems.at[d], (t, partner))

    def og_copy(q, d, place):
        to = other(d)
        return remote(
            og_turned.at[:, to, q],
            og_buf.at[t, q, place],
            send_sems.at[3],
            og_sems.at[q],
            (t, to),
        )

    def along(origin, q, up):
        step = 1 if up else -1
        chunk = og_buf.at[origin, q]
        kind = 0 if up else 1
        return remote(
            chunk, chunk, send_sems.at[4 + kind], z_sems.at[q, origin], (t + step, c)
        )

    def og_start(q):
        og_buf[t, q, c] = og_turned[:, c, q]
        for d in range(1, col_count):
            og_copy(q, d, c).start()

    def og_on(q):
        arrived(og_turned.at[:, 0 : col_count - 1, q], og_sems.at[q])

        @pl.when(t < tok_count - 1)
        def _():
            along(t, q, True).start()

        @pl.when(t > 0)
        def _():
            along(t, q, False).start()

    def relay(q):
        @pl.loop(0, 2 * (tok_count - 1))
        def _(i):
            origin = t + (1 - 2 * lax.rem(i, 2)) * (i // 2 + 1)

            @pl.when((origin >= 0) & (origin < tok_count))
            def _():
                arrived(og_buf.at[origin, q], z_sems.at[q, origin])

                @pl.when((origin < t) & (t < tok_count - 1))
                def _():
                    along(origin, q, True).start()

                @pl.when((origin > t) & (t > 0))
                def _():
                    along(origin, q, False).start()

    def product(q, k):
        rows = col_count * per_home * rows_q
        return jnp.dot(
            og_buf[k, q].reshape(rows, og_buf.shape[5]),
            act_buf[k].reshape(og_buf.shape[5], rows_home),
            preferred_element_type=f32,
        )

    def round_off():
        for r in range(row_blocks):
            piece = total[:, r * B : (r + 1) * B].reshape(col_blocks, per_block, rows_q, B)
            grad[pl.ds(r * col_blocks, col_blocks)] = piece.astype(bf16)

    def pick_piece(o, s):
        owned = table[s, 0, o]
        piece = grad[jnp.maximum(owned - base, 0)]
        return jnp.where(owned >= 0, piece, jnp.zeros_like(piece))

    def g_start(q, d, s):
        to = other(d)
        remote(
            send.at[q, to, s],
            got.at[s, :, c, q],
            send_sems.at[6],
            g_sems.at[q],
            (t, to),
        ).start()

    def last_copy(s, d, place):
        to = other(d)
        return remote(
            send.at[last, to, s],
            got.at[s, :, place, last],
            send_sems.at[6],
            last_sems.at[s],
            (t, to),
        )

    edge = (t == 0) | (t == tok_count - 1)
    early = min(2, chunks)
    og_start(0)
    for d in range(1, tok_count):
        act_copy(t, d).start()
    for q in range(1, chunks):
        og_start(q)
    for q in range(early):
        og_on(q)

    for d in range(1, tok_count):
        act_wait(d)
        for m in range(1, chips):
            share(d, m, chip).start()

    @pl.when(edge)
    def _():
        for q in range(early, chunks):
            og_on(q)

    @pl.loop(0, row_blocks * col_blocks)
    def _(place):
        found = jnp.int32(0)
        for s in range(slots):
            for o in range(col_count):
                found = jnp.where(table[s, 0, o] == base + place, o * slots + s, found)
        pick_ref[place] = found

    @pl.loop(0, chunks)
    def _(q):
        @pl.when(edge | (q == 0))
        def _():
            relay(q)

        @pl.when(q == 0)
        def _():
            for d in range(1, tok_count):
                arrived(act_buf.at[0, 0 : chips - 1, 0], share_sems.at[d])
                to_partner(d, core).start()

        @pl.when(jnp.logical_not(edge))
        def _():
            @pl.when(q + early < chunks)
            def _():
                og_on(q + early)

            @pl.when(q + 1 < chunks)
            def _():
                relay(q + 1)

        @pl.when(q == 0)
        def _():
            own_act.wait()
            for d in range(1, tok_count):
                to_partner(d, 1 - core).wait_recv()

        total[...] = sum(product(q, k) for k in range(tok_count))

        round_off()

        @pl.when(q < last)
        def _():
            @pl.loop(1, col_count)
            def _(d):
                for s in range(slots):
                    send[q, other(d), s] = pick_piece(other(d), s)
                    g_start(q, d, s)

            for s in range(slots):
                got[s, :, c, q] = pick_piece(c, s)

    def last_send(s):
        @pl.loop(1, col_count)
        def _(d):
            send[last, other(d), s] = pick_piece(other(d), s)
            last_copy(s, d, c).start()

        got[s, :, c, last] = pick_piece(c, s)

    first = min(2, slots)

    @pl.loop(0, first)
    def _(s):
        last_send(s)

    @pl.loop(0, last)
    def _(q):
        arrived(send.at[q, 0 : col_count - 1], g_sems.at[q])

    for load in loads:
        load.wait()

    returned = (returned_top, returned_low)

    def back_start(half, s):
        for d in range(1, col_count):
            to = other(d)
            remote(
                back.at[half, s, to],
                returned[half].at[c * slots + s],
                send_sems.at[7],
                back_sems.at[half],
                (t, to),
            ).start()

    held = max(slots - 1, 0)

    @pl.loop(0, slots)
    def _(s):
        arrived(send.at[last, 0 : col_count - 1, s], last_sems.at[s])

        @pl.when(s == 0)
        def _():
            @pl.loop(first, slots)
            def _(later):
                last_send(later)

        decay = jnp.where(table[s, 0, c] >= 0, f32(decay_rate), f32(1.0))
        result, left, right = slot_math(got[s].reshape(B, B), left_out[s], right_out[s], decay)
        for half in range(halves):
            rows = slice(half * (B // halves), (half + 1) * (B // halves))
            back[half, s] = result[rows].reshape(back.shape[2:])
            returned[half][c * slots + s] = back[half, s, c]
        left_out[s] = left
        right_out[s] = right
        back_start(0, s)
        for half in range(1, halves):

            @pl.when(s < held)
            def _():
                back_start(half, s)

    for half in range(1, halves):

        @pl.loop(held, slots)
        def _(s):
            back_start(half, s)

    block_width = width // per_home

    def fill(half, h, target):
        for p in range(per_home):
            piece_at = h * per_home + p
            for r in range(row_blocks):
                place = pick_ref[r * col_blocks + piece_at // per_block]
                block = returned[half][place]
                if per_block > 1:
                    part = lax.rem(piece_at, per_block)
                    parts = [block[:, k * width : (k + 1) * width] for k in range(per_block)]
                    block = parts[0]
                    for k in range(1, per_block):
                        block = jnp.where(part == k, parts[k], block)
                target[r, :, p * block_width : (p + 1) * block_width] = block

    for half in range(halves):
        arrived(returned[half].at[0 : (col_count - 1) * slots], back_sems.at[half])

        @pl.loop(1, col_count)
        def _(d):
            to = other(d)
            fill(half, to, leaving.at[half, to])
            remote(
                leaving.at[half, to],
                home_ref.at[:, half, c],
                send_sems.at[8],
                home_sems.at[0],
                (t, to),
            ).start()

        fill(half, c, home_ref.at[:, half, c])

    gone(act_buf.at[0 : tok_count - 1, 0, 0], send_sems.at[0])
    gone(act_buf.at[0 : tok_count - 1, 0 : chips - 1, 0], send_sems.at[1])
    gone(act_buf.at[0 : tok_count - 1, :, 0], send_sems.at[2])
    gone(og_turned.at[:, 0 : col_count - 1], send_sems.at[3])
    for k in range(tok_count - 1):

        @pl.when(t == k)
        def _():
            gone(og_buf.at[0 : k + 1], send_sems.at[4])

        @pl.when(tok_count - 1 - t == k)
        def _():
            gone(og_buf.at[0 : k + 1], send_sems.at[5])

    gone(send.at[:, 0 : col_count - 1], send_sems.at[6])
    gone(back.at[:, :, 0 : col_count - 1], send_sems.at[7])
    gone(leaving.at[:, 0 : col_count - 1], send_sems.at[8])
    arrived(leaving.at[:, 0 : col_count - 1], home_sems.at[0])


def place_kernel(in_ref, left_ref, right_ref, out_ref, left_out, right_out, sems):
    slots = left_ref.shape[2]
    copies = [pltpu.make_async_copy(in_ref, out_ref, sems.at[0])]
    for s in range(slots):
        for k, (source, target) in enumerate(((left_ref, left_out), (right_ref, right_out))):
            copies.append(
                pltpu.make_async_copy(
                    source.at[0, 0, s], target.at[0, 0, s], sems.at[1 + 2 * s + k]
                )
            )
    for copy in copies:
        copy.start()
    for copy in copies:
        copy.wait()


def per_device(activations, out_grad, owned_blocks, gram_left, gram_right):
    tok_count = lax.axis_size("tok")
    col_count = lax.axis_size("col")
    tok_local, shard_width = out_grad.shape
    rows_home = activations.shape[1] // tok_count
    row_blocks = rows_home // B
    col_blocks = shard_width * col_count // B
    piece_width = min(B, shard_width)
    per_home = shard_width // piece_width
    per_block = B // piece_width
    sub = piece_width // col_count
    chunks = max(1, sub // 16)
    rows_q = sub // chunks
    halves = max(1, min(2, B // col_count // 16))
    back_rows = B // col_count // halves
    slots = owned_blocks.shape[2]
    smem = pl.BlockSpec(memory_space=pltpu.SMEM)

    act = activations.reshape(col_count // 2, 2, tok_local // col_count, activations.shape[1])
    sem = pltpu.SemaphoreType.DMA
    out, left_next, right_next = pl.pallas_call(
        functools.partial(main_kernel, slots),
        out_shape=[
            pltpu.VMEM((row_blocks, halves, col_count, back_rows, shard_width), bf16),
            pltpu.VMEM((slots, B, B), f32),
            pltpu.VMEM((slots, B, B), f32),
        ],
        in_specs=[smem, ANY, ANY, ANY, ANY],
        out_specs=[VMEM, VMEM, VMEM],
        scratch_shapes=[
            pltpu.VMEM((tok_local, shard_width), bf16),
            pltpu.VMEM((per_home, col_count, chunks, rows_q, tok_local), bf16),
            pltpu.VMEM((tok_count, chunks, col_count, per_home, rows_q, tok_local), bf16),
            pltpu.VMEM(
                (tok_count, col_count // 2, 2, tok_local // col_count, rows_home), bf16
            ),
            pltpu.VMEM((col_count * per_home * rows_q, rows_home), f32),
            pltpu.VMEM((row_blocks * col_blocks, per_block, rows_q, B), bf16),
            pltpu.VMEM((chunks, col_count, slots, per_block, rows_q, B), bf16),
            pltpu.VMEM((slots, per_block, col_count, chunks, rows_q, B), bf16),
            pltpu.VMEM((halves, slots, col_count, back_rows, B), bf16),
            pltpu.VMEM((col_count * slots, back_rows, B), bf16),
            pltpu.VMEM((col_count * slots, back_rows, B), bf16),
            pltpu.VMEM((halves, col_count, row_blocks, back_rows, shard_width), bf16),
            pltpu.SMEM((row_blocks * col_blocks,), jnp.int32),
            sem((9,)),
            sem((chunks,)),
            sem((tok_count,)),
            sem((tok_count,)),
            sem((tok_count,)),
            sem((chunks, tok_count)),
            sem((chunks,)),
            sem((slots,)),
            sem((halves,)),
            sem((1,)),
            sem((4,)),
        ],
        compiler_params=pltpu.CompilerParams(
            collective_id=0, has_side_effects=True, vmem_limit_bytes=48 * MIB
        ),
    )(
        owned_blocks.transpose(2, 0, 1),
        *(
            pltpu.with_memory_space_constraint(x, pltpu.HBM)
            for x in (out_grad, act, gram_left[0, 0], gram_right[0, 0])
        ),
    )
    return tuple(
        pl.pallas_call(
            place_kernel,
            out_shape=[
                jax.ShapeDtypeStruct((rows_home, shard_width), bf16),
                jax.ShapeDtypeStruct((1, 1, slots, B, B), f32),
                jax.ShapeDtypeStruct((1, 1, slots, B, B), f32),
            ],
            in_specs=[VMEM, VMEM, VMEM],
            out_specs=[ANY, ANY, ANY],
            scratch_shapes=[pltpu.SemaphoreType.DMA((1 + 2 * slots,))],
            compiler_params=pltpu.CompilerParams(vmem_limit_bytes=16 * MIB),
        )(out.reshape(rows_home, shard_width), left_next[None, None], right_next[None, None])
    )


def solution(mesh):
    in_specs = (
        P("tok", None),
        P("tok", "col"),
        P("tok", None, None),
        P("tok", "col", None, None, None),
        P("tok", "col", None, None, None),
    )
    out_specs = (
        P("tok", "col"),
        P("tok", "col", None, None, None),
        P("tok", "col", None, None, None),
    )
    return jax.shard_map(
        per_device, mesh=mesh, in_specs=in_specs, out_specs=out_specs, check_vma=False
    )
```
